1024 devices in a mesh: row: 64 (over x, y, core), col: 16 (over z).
Axes of the slice: x: 4, y: 8, z: 16, core: 2. Of those that a mesh axis runs over, the one named last changes fastest.
Arguments:
- momentum: float32 [8192, 16384], P('row', 'col'), may hold values from -6 to 6
- right_factor: float32 [16384, 256], P('col'), may hold values from -0.046875 to 0.046875
Outputs:
- new_momentum: float32 [8192, 16384], P('row', 'col')
- update: float32 [8192, 16384], P('row', 'col')
The draws below stay inside these ranges and needn't reach their ends.
All inputs are finite; a program needn't handle non-finite values.
Results may differ from the reference program's by a relative error of at most 0.0001.
Values sent between devices are 32-bit elements; how exact they have to be, the bound alone decides.
A program may use at most 32 MiB of HBM per device.

```python
import math
import jax
import jax.numpy as jnp
from jax import lax

ROWS = 8192
COLS = 16384
RANK = 256
PASSES = 1


def block_levels(stream_key, dims, cuts, least, largest):
    loudness, own = 1.0, jax.random.fold_in(stream_key, 6)
    for axis_at, blocks in cuts:
        draws = jnp.exp(jax.random.uniform(jax.random.fold_in(own, axis_at), (blocks,), jnp.float32, least / len(cuts), largest / len(cuts)))
        loudness = loudness * jnp.repeat(draws, dims[axis_at] // blocks).reshape([-1 if axis == axis_at else 1 for axis in range(len(dims))])
    return loudness


def bell_draw(stream_key, shape, spread, reach, pieces=(), held_as=jnp.bfloat16):
    level = block_levels(stream_key, shape, pieces, -0.22, 0.18) if pieces else 1.0
    values = jax.random.normal(stream_key, shape, jnp.float32) * spread * level
    return jnp.minimum(jnp.maximum(values, -reach), reach).astype(held_as)


def setup_inputs(seed: int = 0) -> dict:
    streams_of = jax.random.split(jax.random.key(seed), 3)
    momentum = bell_draw(streams_of[0], (ROWS, COLS), 1.0, 6.0, ((0, 64), (1, 16)), jnp.float32)
    right_factor = bell_draw(streams_of[1], (COLS, RANK), COLS ** -0.5, 0.046875, ((0, 16),), jnp.float32)
    return {"momentum": momentum, "right_factor": right_factor}


def orthonormal(left_rows, gram_sum):
    lower_tri = jnp.linalg.cholesky(gram_sum)
    return jax.scipy.linalg.solve_triangular(lower_tri, left_rows.T, lower=True).T

def reference(momentum, right_factor):
    highest = lax.Precision.HIGHEST
    factor_q = right_factor
    left_orth = None
    right_full = None
    for turn in range(PASSES):
        left_rows = jnp.dot(momentum, factor_q, precision=highest)
        gram_sum = jnp.dot(left_rows.T, left_rows, precision=highest)
        left_orth = orthonormal(left_rows, gram_sum)
        right_full = jnp.dot(momentum.T, left_orth, precision=highest)
        squares = lax.optimization_barrier(jnp.sum(right_full * right_full, axis=0))
        factor_q = right_full / jnp.sqrt(squares + 1e-06)
    new_momentum = momentum - 0.5 * jnp.dot(left_orth, right_full.T, precision=highest)
    scale = math.sqrt(ROWS * COLS / RANK)
    update = scale * jnp.dot(left_orth, factor_q.T, precision=highest)
    return (new_momentum, update)
```

```python
import functools
import math

import jax
import jax.numpy as jnp
from jax import lax
from jax.experimental import pallas as pl
from jax.experimental.pallas import tpu as pltpu
from jax.sharding import PartitionSpec as P

ROWS = 8192
COLS = 16384
RANK = 256
CORES = 2
Y_CHIPS = 8
BLOCK = 64
HIGHEST = lax.Precision.HIGHEST
MESH = pl.DeviceIdType.MESH

STAGES = (
    "left_rs",
    "left_ag",
    "gram_core",
    "gram_y",
    "gram_x",
    "gram_yag",
    "gram_cag",
    "w_core",
    "w_x",
    "w_y",
    "w_yag",
    "w_xag",
    "w_cag",
    "norm",
)


def dot(a, b, contract=((1,), (0,))):
    return lax.dot_general(
        a, b, (contract, ((), ())), precision=HIGHEST, preferred_element_type=jnp.float32
    )


def invert_cholesky_block(work):
    b = BLOCK
    groups = b // 8
    lanes = 2 * b
    rows8 = lax.broadcasted_iota(jnp.int32, (8, lanes), 0)
    a = [work[8 * g : 8 * g + 8, :] for g in range(groups)]
    pivots = [jnp.ones((8, lanes), jnp.float32) for _ in range(groups)]

    def lane(v, j):
        return jnp.broadcast_to(v[:, j : j + 1], (8, lanes))

    def sub(v, s):
        return jnp.broadcast_to(v[s : s + 1, :], (8, lanes))

    col = [lane(a[g], 0) for g in range(groups)]
    for j in range(b):
        gj, sj = divmod(j, 8)
        pivot = sub(col[gj], sj)
        inv = 1.0 / pivot
        pivots[gj] = jnp.where(rows8 == sj, pivot, pivots[gj])
        if j == b - 1:
            break
        first = (j + 1) // 8
        nxt = {g: lane(a[g], j + 1) for g in range(first, groups)}
        ahead = sub(col[first], (j + 1) % 8) * inv
        row = sub(a[gj], sj) * inv
        new_col = list(col)
        for g in range(first, groups):
            factor = col[g]
            if g == gj:
                factor = jnp.where(rows8 > sj, factor, 0.0)
            new_col[g] = nxt[g] - factor * ahead
            a[g] = a[g] - factor * row
        col = new_col
    out = [a[g] * lax.rsqrt(pivots[g]) for g in range(groups)]
    return jnp.concatenate(out, axis=0)[:, b:]


def kernel(
    sizes,
    m_hbm,
    q_hbm,
    new_hbm,
    upd_hbm,
    m_ref,
    q_ref,
    part,
    left_in,
    left,
    gram_part,
    gram_core,
    gram_half,
    gram_y,
    gram_x,
    gram,
    w_part,
    w_core,
    w_half,
    w_x,
    w_xs,
    w_y,
    w_full,
    norm_in,
    norm_out,
    work,
    right,
    new_ref,
    upd_ref,
    send,
    recv,
    local,
):
    nx, ny, nz, rows, cols, rank = sizes
    row_at = lax.axis_index("row")
    z = lax.axis_index("col")
    c = row_at % CORES
    y = (row_at // CORES) % ny
    x = row_at // (CORES * ny)
    half = rank // 2
    piece = rows // nz
    gpiece = half // ny
    xrows = half // nx
    prow = max(8, xrows // ny)
    csplit = ny * prow // xrows
    pcol = cols // csplit

    def at_z(t):
        return {"col": t}

    def at_y(t):
        return {"row": (x * ny + t) * CORES + c}

    def at_x(t):
        return {"row": (t * ny + y) * CORES + c}

    other = {"row": (x * ny + y) * CORES + (1 - c)}

    def push(stage, src, dst, target):
        s = STAGES.index(stage)
        pltpu.make_async_remote_copy(
            src_ref=src,
            dst_ref=dst,
            send_sem=send.at[s],
            recv_sem=recv.at[s],
            device_id=target,
            device_id_type=MESH,
        ).start()

    def landed(stage, ref):
        pltpu.make_async_copy(ref, ref, recv.at[STAGES.index(stage)]).wait()

    def sent(stage, ref):
        pltpu.make_async_copy(ref, ref, send.at[STAGES.index(stage)]).wait()

    def rows_of(ref, start, size):
        return ref.at[pl.ds(pl.multiple_of(start, 8), size)]

    load_m = pltpu.make_async_copy(m_hbm, m_ref, local.at[0])
    load_q = pltpu.make_async_copy(q_hbm, q_ref, local.at[1])
    load_m.start()
    load_q.start()

    def each(n, fn):
        def body(t, carry):
            fn(t)
            return carry

        lax.fori_loop(1, n, body, 0)

    barrier = pltpu.get_barrier_semaphore()

    def greet(target):
        pl.semaphore_signal(barrier, inc=1, device_id=target, device_id_type=MESH)

    each(nz, lambda t: greet(at_z((z + t) % nz)))
    each(ny, lambda t: greet(at_y((y + t) % ny)))
    each(nx, lambda t: greet(at_x((x + t) % nx)))
    greet(other)
    load_m.wait()
    load_q.wait()
    part[...] = dot(m_ref[...], q_ref[...])
    pl.semaphore_wait(barrier, nz + ny + nx - 3 + 1)

    def far_first(t, n):
        h = t // 2
        return n // 2 + h * (2 * (t % 2) - 1)

    def left_send(t):
        off = far_first(t, nz)
        to = (z + off) % nz
        push("left_rs", rows_of(part, to * piece, piece), rows_of(left_in, (off - 1) * piece, piece), at_z(to))

    each(nz, left_send)
    landed("left_rs", left_in)
    total = part[pl.ds(pl.multiple_of(z * piece, 8), piece), :]
    for t in range(nz - 1):
        total = total + left_in[t * piece : (t + 1) * piece, :]
    left[pl.ds(pl.multiple_of(z * piece, 8), piece), :] = total
    mine = rows_of(left, z * piece, piece)
    each(nz, lambda t: push("left_ag", mine, mine, at_z((z + far_first(t, nz)) % nz)))
    landed("left_ag", left_in)

    left_now = left[...]
    left_t = left_now.T
    gram_part[...] = dot(left_t, left_now)
    push("gram_core", rows_of(gram_part, (1 - c) * half, half), gram_core, other)
    w_part[...] = dot(left_t, m_ref[...])
    push("w_core", rows_of(w_part, (1 - c) * half, half), w_core, other)
    landed("gram_core", gram_core)
    gram_half[...] = gram_part[pl.ds(pl.multiple_of(c * half, 8), half), :] + gram_core[...]

    def gram_y_send(t):
        to = (y + t) % ny
        push("gram_y", rows_of(gram_half, to * gpiece, gpiece), rows_of(gram_y, (t - 1) * gpiece, gpiece), at_y(to))

    each(ny, gram_y_send)
    landed("w_core", w_core)
    w_half[...] = w_part[pl.ds(pl.multiple_of(c * half, 8), half), :] + w_core[...]
    landed("gram_y", gram_y)
    total = gram_half[pl.ds(pl.multiple_of(y * gpiece, 8), gpiece), :]
    for t in range(ny - 1):
        total = total + gram_y[t * gpiece : (t + 1) * gpiece, :]
    gram_x[pl.ds(pl.multiple_of(x * gpiece, 8), gpiece), :] = total
    mine_g = rows_of(gram_x, x * gpiece, gpiece)
    each(nx, lambda t: push("gram_x", mine_g, mine_g, at_x((x + t) % nx)))

    def w_x_send(t):
        to = (x + t) % nx
        push("w_x", rows_of(w_half, to * xrows, xrows), rows_of(w_x, (t - 1) * xrows, xrows), at_x(to))

    each(nx, w_x_send)
    landed("gram_x", gram_x.at[pl.ds(0, (nx - 1) * gpiece)])
    total = gram_x[0:gpiece, :]
    for t in range(1, nx):
        total = total + gram_x[t * gpiece : (t + 1) * gpiece, :]
    at = c * half + y * gpiece
    gram[pl.ds(pl.multiple_of(at, 8), gpiece), :] = total
    mine_a = rows_of(gram, at, gpiece)
    each(ny, lambda t: push("gram_yag", mine_a, mine_a, at_y((y + t) % ny)))
    landed("gram_yag", gram_y)
    mine_h = rows_of(gram, c * half, half)
    push("gram_cag", mine_h, mine_h, other)

    landed("w_x", w_x)
    total = w_half[pl.ds(pl.multiple_of(x * xrows, 8), xrows), :]
    for t in range(nx - 1):
        total = total + w_x[t * xrows : (t + 1) * xrows, :]
    w_xs[...] = total

    def w_piece(ref, base, k):
        return ref.at[
            pl.ds(pl.multiple_of(base + (k // csplit) * prow, 8), prow),
            pl.ds(pl.multiple_of((k % csplit) * pcol, 128), pcol),
        ]

    def w_y_send(t):
        to = (y + t) % ny
        push("w_y", w_piece(w_xs, 0, to), w_y.at[pl.ds(pl.multiple_of((t - 1) * prow, 8), prow)], at_y(to))

    each(ny, w_y_send)
    landed("gram_cag", gram_half)

    nb = rank // BLOCK
    work[...] = gram[...]
    inverse_rows = []
    eye = (
        lax.broadcasted_iota(jnp.int32, (BLOCK, BLOCK), 0) == lax.broadcasted_iota(jnp.int32, (BLOCK, BLOCK), 1)
    ).astype(jnp.float32)
    base_x = c * half + x * xrows

    def after_block(k):
        if k == 0:
            landed("w_y", w_y)
            own = w_xs[
                pl.ds(pl.multiple_of((y // csplit) * prow, 8), prow),
                pl.ds(pl.multiple_of((y % csplit) * pcol, 128), pcol),
            ]
            for t in range(ny - 1):
                own = own + w_y[t * prow : (t + 1) * prow, :]
            w_full[
                pl.ds(pl.multiple_of(base_x + (y // csplit) * prow, 8), prow),
                pl.ds(pl.multiple_of((y % csplit) * pcol, 128), pcol),
            ] = own
            mine_w = w_piece(w_full, base_x, y)
            each(ny, lambda t: push("w_yag", mine_w, mine_w, at_y((y + t) % ny)))
        if k == 1:
            landed("w_yag", w_y)
            mine_x = rows_of(w_full, base_x, xrows)
            each(nx, lambda t: push("w_xag", mine_x, mine_x, at_x((x + t) % nx)))
        if k == 2:
            landed("w_xag", w_x)
            mine_c = rows_of(w_full, c * half, half)
            push("w_cag", mine_c, mine_c, other)

    solved = []
    for k in range(nb):
        lo, hi = k * BLOCK, (k + 1) * BLOCK
        diag = work[lo:hi, lo:hi]
        inv_kk = invert_cholesky_block(jnp.concatenate([diag, eye], axis=1))
        if k == 0:
            inv_row = inv_kk
        else:
            acc = None
            for i in range(k):
                term = dot(solved[i][:, lo - (i + 1) * BLOCK : lo - i * BLOCK], inverse_rows[i], ((0,), (0,)))
                width = (i + 1) * BLOCK
                if width < lo:
                    term = jnp.concatenate([term, jnp.zeros((BLOCK, lo - width), jnp.float32)], axis=1)
                acc = term if acc is None else acc + term
            inv_row = jnp.concatenate([-dot(inv_kk, acc), inv_kk], axis=1)
        inverse_rows.append(inv_row)
        if hi < rank:
            u = dot(inv_kk, work[lo:hi, hi:])
            solved.append(u)
            work[hi:, hi:] = work[hi:, hi:] - dot(u, u, ((0,), (0,)))
        after_block(k)
    inverse = jnp.concatenate(
        [
            r if r.shape[1] == rank else jnp.concatenate([r, jnp.zeros((BLOCK, rank - r.shape[1]), jnp.float32)], axis=1)
            for r in inverse_rows
        ],
        axis=0,
    )
    left_orth = dot(left[...], inverse, ((1,), (1,)))
    landed("w_cag", w_half)
    right[...] = dot(inverse, w_full[...])
    r = right[...]
    ones = jnp.ones((8, cols), jnp.float32)
    squares = dot(ones, r * r, ((1,), (1,)))
    norm_out[...] = squares[0:1, :]
    each(nz, lambda t: push("norm", norm_out, norm_in.at[far_first(t, nz) - 1], at_z((z + far_first(t, nz)) % nz)))
    new_ref[...] = m_ref[...] - dot(0.5 * left_orth, right[...])
    store_new = pltpu.make_async_copy(new_ref, new_hbm, local.at[0])
    store_new.start()
    landed("norm", norm_in)
    total = norm_out[...]
    for t in range(nz - 1):
        total = total + norm_in[t]
    scale = math.sqrt(ROWS * COLS / RANK)
    factor = scale / jnp.sqrt(total + 1e-06)
    upd_ref[...] = dot(left_orth * factor, right[...])
    store_upd = pltpu.make_async_copy(upd_ref, upd_hbm, local.at[1])
    store_upd.start()

    sent("left_rs", left_in)
    sent("left_ag", left_in)
    sent("gram_core", gram_core)
    sent("gram_y", gram_y)
    sent("gram_x", gram_x.at[pl.ds(0, (nx - 1) * gpiece)])
    sent("gram_yag", gram_y)
    sent("gram_cag", gram_half)
    sent("w_core", w_core)
    sent("w_x", w_x)
    sent("w_y", w_y)
    sent("w_yag", w_y)
    sent("w_xag", w_x)
    sent("w_cag", w_half)
    sent("norm", norm_in)
    store_new.wait()
    store_upd.wait()


def local_step(sizes, momentum, right_factor):
    nx, ny, nz, rows, cols, rank = sizes
    half = rank // 2
    piece = rows // nz
    gpiece = half // ny
    xrows = half // nx
    prow = max(8, xrows // ny)
    pcol = cols * xrows // (ny * prow)
    f32 = jnp.float32
    vmem = lambda *shape: pltpu.VMEM(shape, f32)
    out = jax.ShapeDtypeStruct((rows, cols), f32)
    any_spec = pl.BlockSpec(memory_space=pl.ANY)
    return pl.pallas_call(
        functools.partial(kernel, sizes),
        out_shape=(out, out),
        in_specs=[any_spec, any_spec],
        out_specs=(any_spec, any_spec),
        scratch_shapes=[
            vmem(rows, cols),
            vmem(cols, rank),
            vmem(rows, rank),
            vmem(rows - piece, rank),
            vmem(rows, rank),
            vmem(rank, rank),
            vmem(half, rank),
            vmem(half, rank),
            vmem(half - gpiece, rank),
            vmem(nx * gpiece, rank),
            vmem(rank, rank),
            vmem(rank, cols),
            vmem(half, cols),
            vmem(half, cols),
            vmem(half - xrows, cols),
            vmem(xrows, cols),
            vmem((ny - 1) * prow, pcol),
            vmem(rank, cols),
            vmem(nz - 1, 1, rank),
            vmem(1, rank),
            vmem(rank, rank),
            vmem(rank, cols),
            vmem(rows, cols),
            vmem(rows, cols),
            pltpu.SemaphoreType.DMA((len(STAGES),)),
            pltpu.SemaphoreType.DMA((len(STAGES),)),
            pltpu.SemaphoreType.DMA((2,)),
        ],
        compiler_params=pltpu.CompilerParams(collective_id=0, has_side_effects=True, vmem_limit_bytes=40 * 2**20),
        name="dion",
    )(momentum, right_factor)


def solution(mesh):
    nz = mesh.shape["col"]
    ny = Y_CHIPS
    nx = mesh.shape["row"] // (ny * CORES)

    def local(momentum, right_factor):
        sizes = (nx, ny, nz, momentum.shape[0], momentum.shape[1], right_factor.shape[1])
        return local_step(sizes, momentum, right_factor)

    in_specs = (P("row", "col"), P("col", None))
    out_specs = (P("row", "col"), P("row", "col"))
    return jax.shard_map(local, mesh=mesh, in_specs=in_specs, out_specs=out_specs, check_vma=False)
```

```python
import functools
import math

import jax
import jax.numpy as jnp
from jax import lax
from jax.experimental import pallas as pl
from jax.experimental.pallas import tpu as pltpu
from jax.sharding import PartitionSpec as P

ROWS = 8192
COLS = 16384
RANK = 256
CORES = 2
Y_CHIPS = 8
BLOCK = 64
WINDOW = 8
VMEM_BYTES = 67_000_000
HIGHEST = lax.Precision.HIGHEST
MESH = pl.DeviceIdType.MESH

STAGES = (
    "left_rs",
    "left_ag",
    "gram_core",
    "gram_y",
    "gram_x",
    "gram_yag",
    "gram_cag",
    "w_core",
    "wa_x",
    "wa_y",
    "wa_yag",
    "wa_xag",
    "wa_cag",
    "wb_y",
    "wb_x",
    "wb_xag",
    "wb_yag",
    "wb_cag",
    "norm",
)


def dot(a, b, contract=((1,), (0,))):
    return lax.dot_general(
        a, b, (contract, ((), ())), precision=HIGHEST, preferred_element_type=jnp.float32
    )


def invert_cholesky_block(work):
    b = BLOCK
    groups = b // 8
    lanes = 2 * b
    rows8 = lax.broadcasted_iota(jnp.int32, (8, lanes), 0)
    a = [work[8 * g : 8 * g + 8, :] for g in range(groups)]
    pivots = [jnp.ones((8, lanes), jnp.float32) for _ in range(groups)]

    def spread(k):
        return {g: jnp.broadcast_to(a[g][:, k : k + 1], (8, lanes)) for g in range(k // 8, groups)}

    def sub(v, s):
        return jnp.broadcast_to(v[s : s + 1, :], (8, lanes))

    window = {k: spread(k) for k in range(WINDOW)}
    for j in range(b):
        gj, sj = divmod(j, 8)
        col = window.pop(j)
        pivot = sub(col[gj], sj)
        pivots[gj] = jnp.where(rows8 == sj, pivot, pivots[gj])
        if j == b - 1:
            break
        inv = 1.0 / pivot
        factor = {g: col[g] * inv for g in range((j + 1) // 8, groups)}
        for k in range(j + 1, min(j + WINDOW, b)):
            ahead = sub(col[k // 8], k % 8)
            for g in range(k // 8, groups):
                window[k][g] = window[k][g] - factor[g] * ahead
        row = sub(a[gj], sj)
        for g in range((j + 1) // 8, groups):
            f = factor[g]
            if g == gj:
                f = jnp.where(rows8 > sj, f, 0.0)
            a[g] = a[g] - f * row
        if j + WINDOW < b:
            window[j + WINDOW] = spread(j + WINDOW)
    out = [a[g] * lax.rsqrt(pivots[g]) for g in range(groups)]
    return jnp.concatenate(out, axis=0)[:, b:]


class Plan:
    def __init__(self, nx, ny, nz, rows, cols, rank):
        self.nx, self.ny, self.nz = nx, ny, nz
        self.rows, self.cols, self.rank = rows, cols, rank
        self.half = rank // 2
        self.quarter = rank // 4
        self.piece = rows // nz
        self.gpiece = self.half // ny
        self.ax = self.quarter // nx
        self.ay_rows = max(8, self.ax // ny)
        self.ay_split = ny * self.ay_rows // self.ax
        self.ay_cols = cols // self.ay_split
        self.by = self.quarter // ny
        self.bx_cols = cols // nx


def kernel(
    p,
    m_hbm,
    q_hbm,
    new_hbm,
    upd_hbm,
    m_ref,
    q_ref,
    part,
    left_in,
    left,
    gram_part,
    gram_core,
    gram_half,
    gram_y,
    gram_x,
    gram,
    work,
    w_part,
    w_core,
    w_half,
    wa_in,
    wa_sum,
    wa_piece_in,
    wb_in,
    wb_sum,
    wb_piece_in,
    w_full,
    inverse_ref,
    right,
    norm_in,
    norm_out,
    new_ref,
    upd_ref,
    send,
    recv,
    local,
):
    nx, ny, nz, rank = p.nx, p.ny, p.nz, p.rank
    half, quarter, piece, gpiece = p.half, p.quarter, p.piece, p.gpiece
    row_at = lax.axis_index("row")
    z = lax.axis_index("col")
    c = row_at % CORES
    y = (row_at // CORES) % ny
    x = row_at // (CORES * ny)
    other = {"row": (x * ny + y) * CORES + (1 - c)}

    def at_z(t):
        return {"col": t}

    def at_y(t):
        return {"row": (x * ny + t) * CORES + c}

    def at_x(t):
        return {"row": (t * ny + y) * CORES + c}

    def push(stage, src, dst, target):
        s = STAGES.index(stage)
        pltpu.make_async_remote_copy(
            src_ref=src,
            dst_ref=dst,
            send_sem=send.at[s],
            recv_sem=recv.at[s],
            device_id=target,
            device_id_type=MESH,
        ).start()

    def landed(stage, ref):
        pltpu.make_async_copy(ref, ref, recv.at[STAGES.index(stage)]).wait()

    def sent(stage, ref):
        pltpu.make_async_copy(ref, ref, send.at[STAGES.index(stage)]).wait()

    def span(start, size, step=8):
        return pl.ds(pl.multiple_of(start, step), size)

    def rows_of(ref, start, size):
        return ref.at[span(start, size)]

    def far_first(t, n):
        h = t // 2
        return n // 2 + h * (2 * (t % 2) - 1)

    def each(n, fn):
        def body(t, carry):
            fn(far_first(t, n))
            return carry

        lax.fori_loop(1, n, body, 0)

    barrier = pltpu.get_barrier_semaphore()

    def greet(target):
        pl.semaphore_signal(barrier, inc=1, device_id=target, device_id_type=MESH)

    each(nz, lambda t: greet(at_z((z + t) % nz)))
    load_m = pltpu.make_async_copy(m_hbm, m_ref, local.at[0])
    load_q = pltpu.make_async_copy(q_hbm, q_ref, local.at[1])
    load_m.start()
    load_q.start()
    each(ny, lambda t: greet(at_y((y + t) % ny)))
    each(nx, lambda t: greet(at_x((x + t) % nx)))
    greet(other)
    load_m.wait()
    load_q.wait()
    part[...] = dot(m_ref[...], q_ref[...])
    pl.semaphore_wait(barrier, nz + ny + nx - 3 + 1)

    def left_send(t):
        to = (z + t) % nz
        push("left_rs", rows_of(part, to * piece, piece), rows_of(left_in, (t - 1) * piece, piece), at_z(to))

    each(nz, left_send)
    landed("left_rs", left_in)
    total = part[span(z * piece, piece), :]
    for t in range(nz - 1):
        total = total + left_in[t * piece : (t + 1) * piece, :]
    left[span(z * piece, piece), :] = total
    mine = rows_of(left, z * piece, piece)
    each(nz, lambda t: push("left_ag", mine, mine, at_z((z + t) % nz)))
    landed("left_ag", left_in)

    left_now = left[...]
    left_t = work.at[:, 0 : p.rows]
    left_t[...] = left_now.T
    gram_part[...] = dot(left_t[...], left_now)
    push("gram_core", rows_of(gram_part, (1 - c) * half, half), gram_core, other)
    w_part[span((1 - c) * half, half), :] = dot(left_t[span((1 - c) * half, half), :], m_ref[...])
    push("w_core", rows_of(w_part, (1 - c) * half, half), w_core, other)
    landed("gram_core", gram_core)
    gram_half[...] = gram_part[span(c * half, half), :] + gram_core[...]

    def gram_y_send(t):
        to = (y + t) % ny
        push("gram_y", rows_of(gram_half, to * gpiece, gpiece), rows_of(gram_y, (t - 1) * gpiece, gpiece), at_y(to))

    each(ny, gram_y_send)
    w_half[...] = dot(left_t[span(c * half, half), :], m_ref[...])
    landed("w_core", w_core)
    w_half[...] = w_half[...] + w_core[...]

    def wa_x_send(t):
        to = (x + t) % nx
        push("wa_x", rows_of(w_half, to * p.ax, p.ax), rows_of(wa_in, (t - 1) * p.ax, p.ax), at_x(to))

    def wb_y_send(t):
        to = (y + t) % ny
        push("wb_y", rows_of(w_half, quarter + to * p.by, p.by), rows_of(wb_in, (t - 1) * p.by, p.by), at_y(to))

    each(nx, wa_x_send)
    each(ny, wb_y_send)
    landed("gram_y", gram_y)
    total = gram_half[span(y * gpiece, gpiece), :]
    for t in range(ny - 1):
        total = total + gram_y[t * gpiece : (t + 1) * gpiece, :]
    gram_x[span(x * gpiece, gpiece), :] = total
    mine_g = rows_of(gram_x, x * gpiece, gpiece)
    each(nx, lambda t: push("gram_x", mine_g, mine_g, at_x((x + t) % nx)))
    landed("gram_x", gram_x.at[pl.ds(0, (nx - 1) * gpiece)])
    total = gram_x[0:gpiece, :]
    for t in range(1, nx):
        total = total + gram_x[t * gpiece : (t + 1) * gpiece, :]
    at = c * half + y * gpiece
    gram[span(at, gpiece), :] = total
    mine_a = rows_of(gram, at, gpiece)
    each(ny, lambda t: push("gram_yag", mine_a, mine_a, at_y((y + t) % ny)))

    def a_piece(ref, base, k):
        return ref.at[
            span(base + (k // p.ay_split) * p.ay_rows, p.ay_rows),
            span((k % p.ay_split) * p.ay_cols, p.ay_cols, 128),
        ]

    def wa_y_send(t):
        to = (y + t) % ny
        push("wa_y", a_piece(wa_sum, 0, to), rows_of(wa_piece_in, (t - 1) * p.ay_rows, p.ay_rows), at_y(to))

    landed("wa_x", wa_in)
    total = w_half[span(x * p.ax, p.ax), :]
    for t in range(nx - 1):
        total = total + wa_in[t * p.ax : (t + 1) * p.ax, :]
    wa_sum[...] = total
    each(ny, wa_y_send)

    def b_piece(ref, base, k):
        return ref.at[span(base, p.by), span(k * p.bx_cols, p.bx_cols, 128)]

    def wb_x_send(t):
        to = (x + t) % nx
        push("wb_x", b_piece(wb_sum, 0, to), rows_of(wb_piece_in, (t - 1) * p.by, p.by), at_x(to))

    landed("wb_y", wb_in)
    total = w_half[span(quarter + y * p.by, p.by), :]
    for t in range(ny - 1):
        total = total + wb_in[t * p.by : (t + 1) * p.by, :]
    wb_sum[...] = total
    each(nx, wb_x_send)

    landed("gram_yag", gram_y)
    mine_h = rows_of(gram, c * half, half)
    push("gram_cag", mine_h, mine_h, other)

    base_a = c * half + x * p.ax
    base_b = c * half + quarter + y * p.by
    landed("wb_x", wb_piece_in)
    total = b_piece(wb_sum, 0, x)[...]
    for t in range(nx - 1):
        total = total + wb_piece_in[t * p.by : (t + 1) * p.by, :]
    mine_b = b_piece(w_full, base_b, x)
    mine_b[...] = total
    each(nx, lambda t: push("wb_xag", mine_b, mine_b, at_x((x + t) % nx)))
    landed("wa_y", wa_piece_in)
    total = a_piece(wa_sum, 0, y)[...]
    for t in range(ny - 1):
        total = total + wa_piece_in[t * p.ay_rows : (t + 1) * p.ay_rows, :]
    mine_w = a_piece(w_full, base_a, y)
    mine_w[...] = total
    each(ny, lambda t: push("wa_yag", mine_w, mine_w, at_y((y + t) % ny)))
    landed("gram_cag", gram_half)

    nb = rank // BLOCK
    work[...] = gram[...]
    eye = (
        lax.broadcasted_iota(jnp.int32, (BLOCK, BLOCK), 0) == lax.broadcasted_iota(jnp.int32, (BLOCK, BLOCK), 1)
    ).astype(jnp.float32)

    def after_block(k):
        if k == 0:
            landed("wb_xag", wb_piece_in)
            rows_b = rows_of(w_full, base_b, p.by)
            each(ny, lambda t: push("wb_yag", rows_b, rows_b, at_y((y + t) % ny)))
        if k == 1:
            landed("wa_yag", wa_piece_in)
            rows_a = rows_of(w_full, base_a, p.ax)
            each(nx, lambda t: push("wa_xag", rows_a, rows_a, at_x((x + t) % nx)))

    inverse_rows = []
    solved = []
    for k in range(nb):
        lo, hi = k * BLOCK, (k + 1) * BLOCK
        diag = work[lo:hi, lo:hi]
        inv_kk = invert_cholesky_block(jnp.concatenate([diag, eye], axis=1))
        if hi < rank:
            u = dot(inv_kk, work[lo:hi, hi:])
            solved.append(u)
            work[hi:, hi:] = work[hi:, hi:] - dot(u, u, ((0,), (0,)))
        inv_row = inv_kk
        if k > 0:
            acc = None
            for i in range(k):
                term = dot(solved[i][:, lo - (i + 1) * BLOCK : lo - i * BLOCK], inverse_rows[i], ((0,), (0,)))
                width = (i + 1) * BLOCK
                if width < lo:
                    term = jnp.concatenate([term, jnp.zeros((BLOCK, lo - width), jnp.float32)], axis=1)
                acc = term if acc is None else acc + term
            inv_row = jnp.concatenate([-dot(inv_kk, acc), inv_kk], axis=1)
        inverse_rows.append(inv_row)
        if hi < rank:
            inv_row = jnp.concatenate([inv_row, jnp.zeros((BLOCK, rank - hi), jnp.float32)], axis=1)
        inverse_ref[lo:hi, :] = inv_row
        after_block(k)
    left_orth = dot(left[...], inverse_ref[...], ((1,), (1,)))
    landed("wa_xag", wa_in)
    rows_a2 = rows_of(w_full, c * half, quarter)
    push("wa_cag", rows_a2, rows_a2, other)
    landed("wb_yag", wb_in)
    rows_b2 = rows_of(w_full, c * half + quarter, quarter)
    push("wb_cag", rows_b2, rows_b2, other)
    right[...] = dot(inverse_ref[:, span(c * half, half, 128)], w_full[span(c * half, half), :])
    landed("wa_cag", w_core.at[pl.ds(0, quarter)])
    landed("wb_cag", w_core.at[pl.ds(0, quarter)])
    r = right[...] + dot(inverse_ref[:, span((1 - c) * half, half, 128)], w_full[span((1 - c) * half, half), :])
    right[...] = r
    folded = r[:, 0:128] * r[:, 0:128]
    for t in range(1, p.cols // 128):
        folded = folded + r[:, 128 * t : 128 * (t + 1)] * r[:, 128 * t : 128 * (t + 1)]
    squares = dot(jnp.ones((8, 128), jnp.float32), folded, ((1,), (1,)))
    norm_out[...] = squares[0:1, :]
    each(nz, lambda t: push("norm", norm_out, norm_in.at[t - 1], at_z((z + t) % nz)))
    new_ref[...] = m_ref[...] - dot(0.5 * left_orth, right[...])
    store_new = pltpu.make_async_copy(new_ref, new_hbm, local.at[0])
    store_new.start()
    landed("norm", norm_in)
    total = norm_out[...]
    for t in range(nz - 1):
        total = total + norm_in[t]
    scale = math.sqrt(ROWS * COLS / RANK)
    factor = scale / jnp.sqrt(total + 1e-06)
    upd_ref[...] = dot(left_orth * factor, right[...])
    store_upd = pltpu.make_async_copy(upd_ref, upd_hbm, local.at[1])
    store_upd.start()

    sent("left_rs", left_in)
    sent("left_ag", left_in)
    sent("gram_core", gram_core)
    sent("gram_y", gram_y)
    sent("gram_x", gram_x.at[pl.ds(0, (nx - 1) * gpiece)])
    sent("gram_yag", gram_y)
    sent("gram_cag", gram_half)
    sent("w_core", w_core)
    sent("wa_x", wa_in)
    sent("wa_y", wa_piece_in)
    sent("wa_yag", wa_piece_in)
    sent("wa_xag", wa_in)
    sent("wa_cag", w_core.at[pl.ds(0, quarter)])
    sent("wb_y", wb_in)
    sent("wb_x", wb_piece_in)
    sent("wb_xag", wb_piece_in)
    sent("wb_yag", wb_in)
    sent("wb_cag", w_core.at[pl.ds(0, quarter)])
    sent("norm", norm_in)
    store_new.wait()
    store_upd.wait()


def local_step(p, momentum, right_factor):
    f32 = jnp.float32
    vmem = lambda *shape: pltpu.VMEM(shape, f32)
    out = jax.ShapeDtypeStruct((p.rows, p.cols), f32)
    any_spec = pl.BlockSpec(memory_space=pl.ANY)
    return pl.pallas_call(
        functools.partial(kernel, p),
        out_shape=(out, out),
        in_specs=[any_spec, any_spec],
        out_specs=(any_spec, any_spec),
        scratch_shapes=[
            vmem(p.rows, p.cols),
            vmem(p.cols, p.rank),
            vmem(p.rows, p.rank),
            vmem(p.rows - p.piece, p.rank),
            vmem(p.rows, p.rank),
            vmem(p.rank, p.rank),
            vmem(p.half, p.rank),
            vmem(p.half, p.rank),
            vmem(p.half - p.gpiece, p.rank),
            vmem(p.nx * p.gpiece, p.rank),
            vmem(p.rank, p.rank),
            vmem(p.rank, p.rank),
            vmem(p.rank, p.cols),
            vmem(p.half, p.cols),
            vmem(p.half, p.cols),
            vmem(p.quarter - p.ax, p.cols),
            vmem(p.ax, p.cols),
            vmem((p.ny - 1) * p.ay_rows, p.ay_cols),
            vmem(p.quarter - p.by, p.cols),
            vmem(p.by, p.cols),
            vmem((p.nx - 1) * p.by, p.bx_cols),
            vmem(p.rank, p.cols),
            vmem(p.rank, p.rank),
            vmem(p.rank, p.cols),
            vmem(p.nz - 1, 1, p.rank),
            vmem(1, p.rank),
            vmem(p.rows, p.cols),
            vmem(p.rows, p.cols),
            pltpu.SemaphoreType.DMA((len(STAGES),)),
            pltpu.SemaphoreType.DMA((len(STAGES),)),
            pltpu.SemaphoreType.DMA((2,)),
        ],
        compiler_params=pltpu.CompilerParams(collective_id=0, has_side_effects=True, vmem_limit_bytes=VMEM_BYTES),
        name="dion",
    )(momentum, right_factor)


def solution(mesh):
    nz = mesh.shape["col"]
    ny = Y_CHIPS
    nx = mesh.shape["row"] // (ny * CORES)

    def local(momentum, right_factor):
        plan = Plan(nx, ny, nz, momentum.shape[0], momentum.shape[1], right_factor.shape[1])
        return local_step(plan, momentum, right_factor)

    in_specs = (P("row", "col"), P("col", None))
    out_specs = (P("row", "col"), P("row", "col"))
    return jax.shard_map(local, mesh=mesh, in_specs=in_specs, out_specs=out_specs, check_vma=False)
```

```python
import functools
import math

import jax
import jax.numpy as jnp
from jax import lax
from jax.experimental import pallas as pl
from jax.experimental.pallas import tpu as pltpu
from jax.sharding import PartitionSpec as P

ROWS = 8192
COLS = 16384
RANK = 256
CORES = 2
Y_CHIPS = 8
BLOCK = 64
WINDOW = 8
VMEM_BYTES = 24 * 2**20
HIGHEST = lax.Precision.HIGHEST
MESH = pl.DeviceIdType.MESH

STAGES = (
    "left_rs",
    "left_ag",
    "gram_core",
    "gram_y",
    "gram_x",
    "gram_yag",
    "gram_cag",
    "w_core",
    "wa_x",
    "wa_y",
    "wa_yag",
    "wa_xag",
    "wb_y",
    "wb_x",
    "wb_xag",
    "wb_yag",
    "right_core",
    "norm",
)


def dot(a, b, contract=((1,), (0,))):
    return lax.dot_general(
        a, b, (contract, ((), ())), precision=HIGHEST, preferred_element_type=jnp.float32
    )


def invert_cholesky_block(work):
    b = BLOCK
    groups = b // 8
    lanes = 2 * b
    rows8 = lax.broadcasted_iota(jnp.int32, (8, lanes), 0)
    a = [work[8 * g : 8 * g + 8, :] for g in range(groups)]
    pivots = [jnp.ones((8, lanes), jnp.float32) for _ in range(groups)]

    def spread(k):
        return {g: jnp.broadcast_to(a[g][:, k : k + 1], (8, lanes)) for g in range(k // 8, groups)}

    def sub(v, s):
        return jnp.broadcast_to(v[s : s + 1, :], (8, lanes))

    window = {k: spread(k) for k in range(WINDOW)}
    for j in range(b):
        gj, sj = divmod(j, 8)
        col = window.pop(j)
        pivot = sub(col[gj], sj)
        pivots[gj] = jnp.where(rows8 == sj, pivot, pivots[gj])
        if j == b - 1:
            break
        inv = 1.0 / pivot
        factor = {g: col[g] * inv for g in range((j + 1) // 8, groups)}
        for k in range(j + 1, min(j + WINDOW, b)):
            ahead = sub(col[k // 8], k % 8)
            for g in range(k // 8, groups):
                window[k][g] = window[k][g] - factor[g] * ahead
        row = sub(a[gj], sj)
        for g in range((j + 1) // 8, groups):
            f = factor[g]
            if g == gj:
                f = jnp.where(rows8 > sj, f, 0.0)
            a[g] = a[g] - f * row
        if j + WINDOW < b:
            window[j + WINDOW] = spread(j + WINDOW)
    out = [a[g] * lax.rsqrt(pivots[g]) for g in range(groups)]
    return jnp.concatenate(out, axis=0)[:, b:]


class Plan:
    def __init__(self, nx, ny, nz, rows, cols, rank):
        self.nx, self.ny, self.nz = nx, ny, nz
        self.rows, self.cols, self.rank = rows, cols, rank
        self.half = rank // 2
        self.hcols = cols // 2
        self.piece = rows // nz
        self.gpiece = self.half // ny
        self.ax = self.half // nx
        self.ay_rows = max(8, self.ax // ny)
        self.ay_split = ny * self.ay_rows // self.ax
        self.ay_cols = self.hcols // self.ay_split
        self.by = self.half // ny
        self.bx_rows = max(8, self.by // nx)
        self.bx_split = nx * self.bx_rows // self.by
        self.bx_cols = self.hcols // self.bx_split


def kernel(
    p,
    m_hbm,
    q_hbm,
    new_out,
    right_out,
    left_out,
    m_ref,
    q_ref,
    part,
    left_in,
    left,
    gram_part,
    gram_core,
    gram_half,
    gram_y,
    gram_x,
    gram,
    work,
    w_part,
    w_core,
    w_half,
    wa_in,
    wa_sum,
    wa_piece_in,
    wb_in,
    wb_sum,
    wb_piece_in,
    w_full,
    inverse_ref,
    right,
    norm_in,
    norm_out,
    send,
    recv,
    local,
):
    nx, ny, nz, rank = p.nx, p.ny, p.nz, p.rank
    half, hcols, piece, gpiece = p.half, p.hcols, p.piece, p.gpiece
    row_at = lax.axis_index("row")
    z = lax.axis_index("col")
    c = row_at % CORES
    y = (row_at // CORES) % ny
    x = row_at // (CORES * ny)
    other_row = (x * ny + y) * CORES + (1 - c)
    other = {"row": other_row}

    def at_z(t):
        return {"col": t}

    def at_z_other(t):
        return {"row": other_row, "col": t}

    def at_y(t):
        return {"row": (x * ny + t) * CORES + c}

    def at_x(t):
        return {"row": (t * ny + y) * CORES + c}

    def push(stage, src, dst, target):
        s = STAGES.index(stage)
        pltpu.make_async_remote_copy(
            src_ref=src,
            dst_ref=dst,
            send_sem=send.at[s],
            recv_sem=recv.at[s],
            device_id=target,
            device_id_type=MESH,
        ).start()

    def landed(stage, ref):
        pltpu.make_async_copy(ref, ref, recv.at[STAGES.index(stage)]).wait()

    def sent(stage, ref):
        pltpu.make_async_copy(ref, ref, send.at[STAGES.index(stage)]).wait()

    def span(start, size, step=8):
        return pl.ds(pl.multiple_of(start, step), size)

    def rows_of(ref, start, size):
        return ref.at[span(start, size)]

    def far_first(t, n):
        h = t // 2
        return n // 2 + h * (2 * (t % 2) - 1)

    def each(n, fn):
        def body(t, carry):
            fn(far_first(t, n))
            return carry

        lax.fori_loop(1, n, body, 0)

    barrier = pltpu.get_barrier_semaphore()

    def greet(target):
        pl.semaphore_signal(barrier, inc=1, device_id=target, device_id_type=MESH)

    each(nz, lambda t: greet(at_z((z + t) % nz)))
    load_m = pltpu.make_async_copy(m_hbm, m_ref, local.at[0])
    load_q = pltpu.make_async_copy(q_hbm, q_ref, local.at[1])
    load_m.start()
    load_q.start()
    each(ny, lambda t: greet(at_y((y + t) % ny)))
    each(nx, lambda t: greet(at_x((x + t) % nx)))
    each(nz, lambda t: greet(at_z_other((z + t) % nz)))
    greet(other)
    load_m.wait()
    load_q.wait()
    part[...] = dot(m_ref[...], q_ref[...])
    pl.semaphore_wait(barrier, 2 * nz + ny + nx - 3)

    def left_send(t):
        to = (z + t) % nz
        push("left_rs", rows_of(part, to * piece, piece), rows_of(left_in, (t - 1) * piece, piece), at_z(to))

    each(nz, left_send)
    landed("left_rs", left_in)
    total = part[span(z * piece, piece), :]
    for t in range(nz - 1):
        total = total + left_in[t * piece : (t + 1) * piece, :]
    left[span(z * piece, piece), :] = total
    mine = rows_of(left, z * piece, piece)
    each(nz, lambda t: push("left_ag", mine, mine, at_z((z + t) % nz)))
    landed("left_ag", left_in)

    left_now = left[...]
    left_t = work.at[:, 0 : p.rows]
    left_t[...] = left_now.T
    gram_part[...] = dot(left_t[...], left_now)
    push("gram_core", rows_of(gram_part, (1 - c) * half, half), gram_core, other)
    w_part[...] = dot(left_t[...], m_ref[:, span((1 - c) * hcols, hcols, 128)])
    push("w_core", w_part, w_core, other)
    landed("gram_core", gram_core)
    gram_half[...] = gram_part[span(c * half, half), :] + gram_core[...]

    def gram_y_send(t):
        to = (y + t) % ny
        push("gram_y", rows_of(gram_half, to * gpiece, gpiece), rows_of(gram_y, (t - 1) * gpiece, gpiece), at_y(to))

    each(ny, gram_y_send)
    w_half[...] = dot(left_t[...], m_ref[:, span(c * hcols, hcols, 128)])
    landed("w_core", w_core)
    w_half[...] = w_half[...] + w_core[...]

    def wa_x_send(t):
        to = (x + t) % nx
        push("wa_x", rows_of(w_half, to * p.ax, p.ax), rows_of(wa_in, (t - 1) * p.ax, p.ax), at_x(to))

    def wb_y_send(t):
        to = (y + t) % ny
        push("wb_y", rows_of(w_half, half + to * p.by, p.by), rows_of(wb_in, (t - 1) * p.by, p.by), at_y(to))

    each(nx, wa_x_send)
    each(ny, wb_y_send)
    landed("gram_y", gram_y)
    total = gram_half[span(y * gpiece, gpiece), :]
    for t in range(ny - 1):
        total = total + gram_y[t * gpiece : (t + 1) * gpiece, :]
    gram_x[span(x * gpiece, gpiece), :] = total
    mine_g = rows_of(gram_x, x * gpiece, gpiece)
    each(nx, lambda t: push("gram_x", mine_g, mine_g, at_x((x + t) % nx)))
    landed("gram_x", gram_x.at[pl.ds(0, (nx - 1) * gpiece)])
    total = gram_x[0:gpiece, :]
    for t in range(1, nx):
        total = total + gram_x[t * gpiece : (t + 1) * gpiece, :]
    at = c * half + y * gpiece
    gram[span(at, gpiece), :] = total
    mine_a = rows_of(gram, at, gpiece)
    each(ny, lambda t: push("gram_yag", mine_a, mine_a, at_y((y + t) % ny)))

    def a_piece(ref, base, k):
        return ref.at[
            span(base + (k // p.ay_split) * p.ay_rows, p.ay_rows),
            span((k % p.ay_split) * p.ay_cols, p.ay_cols, 128),
        ]

    def b_piece(ref, base, k):
        return ref.at[
            span(base + (k // p.bx_split) * p.bx_rows, p.bx_rows),
            span((k % p.bx_split) * p.bx_cols, p.bx_cols, 128),
        ]

    def wa_y_send(t):
        to = (y + t) % ny
        push("wa_y", a_piece(wa_sum, 0, to), rows_of(wa_piece_in, (t - 1) * p.ay_rows, p.ay_rows), at_y(to))

    landed("wa_x", wa_in)
    total = w_half[span(x * p.ax, p.ax), :]
    for t in range(nx - 1):
        total = total + wa_in[t * p.ax : (t + 1) * p.ax, :]
    wa_sum[...] = total
    each(ny, wa_y_send)

    def wb_x_send(t):
        to = (x + t) % nx
        push("wb_x", b_piece(wb_sum, 0, to), rows_of(wb_piece_in, (t - 1) * p.bx_rows, p.bx_rows), at_x(to))

    landed("wb_y", wb_in)
    total = w_half[span(half + y * p.by, p.by), :]
    for t in range(ny - 1):
        total = total + wb_in[t * p.by : (t + 1) * p.by, :]
    wb_sum[...] = total
    each(nx, wb_x_send)

    landed("gram_yag", gram_y)
    mine_h = rows_of(gram, c * half, half)
    push("gram_cag", mine_h, mine_h, other)

    base_a = x * p.ax
    base_b = half + y * p.by
    landed("wb_x", wb_piece_in)
    total = b_piece(wb_sum, 0, x)[...]
    for t in range(nx - 1):
        total = total + wb_piece_in[t * p.bx_rows : (t + 1) * p.bx_rows, :]
    mine_b = b_piece(w_full, base_b, x)
    mine_b[...] = total
    each(nx, lambda t: push("wb_xag", mine_b, mine_b, at_x((x + t) % nx)))
    landed("wa_y", wa_piece_in)
    total = a_piece(wa_sum, 0, y)[...]
    for t in range(ny - 1):
        total = total + wa_piece_in[t * p.ay_rows : (t + 1) * p.ay_rows, :]
    mine_w = a_piece(w_full, base_a, y)
    mine_w[...] = total
    each(ny, lambda t: push("wa_yag", mine_w, mine_w, at_y((y + t) % ny)))
    landed("gram_cag", gram_half)

    nb = rank // BLOCK
    work[...] = gram[...]
    eye = (
        lax.broadcasted_iota(jnp.int32, (BLOCK, BLOCK), 0) == lax.broadcasted_iota(jnp.int32, (BLOCK, BLOCK), 1)
    ).astype(jnp.float32)

    def after_block(k):
        if k == 0:
            landed("wb_xag", wb_piece_in)
            rows_b = rows_of(w_full, base_b, p.by)
            each(ny, lambda t: push("wb_yag", rows_b, rows_b, at_y((y + t) % ny)))
        if k == 1:
            landed("wa_yag", wa_piece_in)
            rows_a = rows_of(w_full, base_a, p.ax)
            each(nx, lambda t: push("wa_xag", rows_a, rows_a, at_x((x + t) % nx)))

    inverse_rows = []
    solved = []
    for k in range(nb):
        lo, hi = k * BLOCK, (k + 1) * BLOCK
        diag = work[lo:hi, lo:hi]
        inv_kk = invert_cholesky_block(jnp.concatenate([diag, eye], axis=1))
        if hi < rank:
            u = dot(inv_kk, work[lo:hi, hi:])
            solved.append(u)
            work[hi:, hi:] = work[hi:, hi:] - dot(u, u, ((0,), (0,)))
        inv_row = inv_kk
        if k > 0:
            acc = None
            for i in range(k):
                term = dot(solved[i][:, lo - (i + 1) * BLOCK : lo - i * BLOCK], inverse_rows[i], ((0,), (0,)))
                width = (i + 1) * BLOCK
                if width < lo:
                    term = jnp.concatenate([term, jnp.zeros((BLOCK, lo - width), jnp.float32)], axis=1)
                acc = term if acc is None else acc + term
            inv_row = jnp.concatenate([-dot(inv_kk, acc), inv_kk], axis=1)
        inverse_rows.append(inv_row)
        if hi < rank:
            inv_row = jnp.concatenate([inv_row, jnp.zeros((BLOCK, rank - hi), jnp.float32)], axis=1)
        inverse_ref[lo:hi, :] = inv_row
        after_block(k)
    left_orth = dot(left[...], inverse_ref[...], ((1,), (1,)))
    landed("wa_xag", wa_in)
    landed("wb_yag", wb_in)
    r = dot(inverse_ref[...], w_full[...])
    right[c] = r
    push("right_core", right.at[c], right.at[c], other)
    folded = r[:, 0:128] * r[:, 0:128]
    for t in range(1, hcols // 128):
        folded = folded + r[:, 128 * t : 128 * (t + 1)] * r[:, 128 * t : 128 * (t + 1)]
    squares = dot(jnp.ones((8, 128), jnp.float32), folded, ((1,), (1,)))
    norm_out[...] = squares[0:1, :]

    def norm_send(t):
        to = (z + t) % nz
        push("norm", norm_out, norm_in.at[t - 1], at_z(to))
        push("norm", norm_out, norm_in.at[nz - 1 + t], at_z_other(to))

    each(nz, norm_send)
    push("norm", norm_out, norm_in.at[nz - 1], other)
    half_orth = 0.5 * left_orth
    mine_cols = span(c * hcols, hcols, 128)
    new_out[:, mine_cols] = m_ref[:, mine_cols] - dot(half_orth, right[c])
    landed("right_core", w_half)
    other_cols = span((1 - c) * hcols, hcols, 128)
    new_out[:, other_cols] = m_ref[:, other_cols] - dot(half_orth, right[1 - c])
    right_out[...] = right[...]
    landed("norm", norm_in)
    total = norm_out[...]
    for t in range(2 * nz - 1):
        total = total + norm_in[t]
    scale = math.sqrt(ROWS * COLS / RANK)
    left_out[...] = left_orth * (scale / jnp.sqrt(total + 1e-06))

    sent("left_rs", left_in)
    sent("left_ag", left_in)
    sent("gram_core", gram_core)
    sent("gram_y", gram_y)
    sent("gram_x", gram_x.at[pl.ds(0, (nx - 1) * gpiece)])
    sent("gram_yag", gram_y)
    sent("gram_cag", gram_half)
    sent("w_core", w_core)
    sent("wa_x", wa_in)
    sent("wa_y", wa_piece_in)
    sent("wa_yag", wa_piece_in)
    sent("wa_xag", wa_in)
    sent("wb_y", wb_in)
    sent("wb_x", wb_piece_in)
    sent("wb_xag", wb_piece_in)
    sent("wb_yag", wb_in)
    sent("right_core", w_half)
    sent("norm", norm_in)


def write_outputs(new_ref, right_ref, left_ref, new_hbm, upd_hbm, upd, sems):
    hcols = right_ref.shape[2]
    copies = [pltpu.make_async_copy(new_ref, new_hbm, sems.at[0])]
    copies[0].start()
    for h in range(2):
        at = pl.ds(h * hcols, hcols)
        upd[:, at] = dot(left_ref[...], right_ref[h])
        copies.append(pltpu.make_async_copy(upd.at[:, at], upd_hbm.at[:, at], sems.at[1 + h]))
        copies[-1].start()
    for copy in copies:
        copy.wait()


def local_step(p, momentum, right_factor):
    f32 = jnp.float32
    vmem = lambda *shape: pltpu.VMEM(shape, f32)
    shaped = lambda *shape: jax.ShapeDtypeStruct(shape, f32)
    any_spec = pl.BlockSpec(memory_space=pl.ANY)
    hbm_spec = pl.BlockSpec(memory_space=pltpu.HBM)
    vmem_spec = pl.BlockSpec(memory_space=pltpu.VMEM)
    new, right, left = pl.pallas_call(
        functools.partial(kernel, p),
        out_shape=(shaped(p.rows, p.cols), shaped(2, p.rank, p.hcols), shaped(p.rows, p.rank)),
        in_specs=[hbm_spec, hbm_spec],
        out_specs=(vmem_spec,) * 3,
        scratch_shapes=[
            vmem(p.rows, p.cols),
            vmem(p.cols, p.rank),
            vmem(p.rows, p.rank),
            vmem(p.rows - p.piece, p.rank),
            vmem(p.rows, p.rank),
            vmem(p.rank, p.rank),
            vmem(p.half, p.rank),
            vmem(p.half, p.rank),
            vmem(p.half - p.gpiece, p.rank),
            vmem(p.nx * p.gpiece, p.rank),
            vmem(p.rank, p.rank),
            vmem(p.rank, p.rank),
            vmem(p.rank, p.hcols),
            vmem(p.rank, p.hcols),
            vmem(p.rank, p.hcols),
            vmem(p.half - p.ax, p.hcols),
            vmem(p.ax, p.hcols),
            vmem((p.ny - 1) * p.ay_rows, p.ay_cols),
            vmem(p.half - p.by, p.hcols),
            vmem(p.by, p.hcols),
            vmem((p.nx - 1) * p.bx_rows, p.bx_cols),
            vmem(p.rank, p.hcols),
            vmem(p.rank, p.rank),
            vmem(2, p.rank, p.hcols),
            vmem(2 * p.nz - 1, 1, p.rank),
            vmem(1, p.rank),
            pltpu.SemaphoreType.DMA((len(STAGES),)),
            pltpu.SemaphoreType.DMA((len(STAGES),)),
            pltpu.SemaphoreType.DMA((2,)),
        ],
        compiler_params=pltpu.CompilerParams(collective_id=0, has_side_effects=True, vmem_limit_bytes=VMEM_BYTES),
        name="dion",
    )(
        pltpu.with_memory_space_constraint(momentum, pltpu.HBM),
        pltpu.with_memory_space_constraint(right_factor, pltpu.HBM),
    )
    return pl.pallas_call(
        write_outputs,
        out_shape=(shaped(p.rows, p.cols),) * 2,
        in_specs=[vmem_spec] * 3,
        out_specs=(any_spec, any_spec),
        scratch_shapes=[vmem(p.rows, p.cols), pltpu.SemaphoreType.DMA((3,))],
        compiler_params=pltpu.CompilerParams(vmem_limit_bytes=8 * 2**20),
        name="outputs",
    )(new, right, left)


def solution(mesh):
    nz = mesh.shape["col"]
    ny = Y_CHIPS
    nx = mesh.shape["row"] // (ny * CORES)

    def local(momentum, right_factor):
        plan = Plan(nx, ny, nz, momentum.shape[0], momentum.shape[1], right_factor.shape[1])
        return local_step(plan, momentum, right_factor)

    in_specs = (P("row", "col"), P("col", None))
    out_specs = (P("row", "col"), P("row", "col"))
    return jax.shard_map(local, mesh=mesh, in_specs=in_specs, out_specs=out_specs, check_vma=False)
```

```python
import functools
import math

import jax
import jax.numpy as jnp
from jax import lax
from jax.experimental import pallas as pl
from jax.experimental.pallas import tpu as pltpu
from jax.sharding import PartitionSpec as P

ROWS = 8192
COLS = 16384
RANK = 256
CORES = 2
Y_CHIPS = 8
BLOCK = 64
WINDOW = 8
VMEM_BYTES = 24 * 2**20
HIGHEST = lax.Precision.HIGHEST
MESH = pl.DeviceIdType.MESH

A_CHUNKS = 3
STAGES = (
    ("left_rs", "left_ag", "gram_core", "gram_y", "gram_x", "gram_yag", "gram_cag", "w_core")
    + tuple(f"wa{i}_{s}" for i in range(A_CHUNKS) for s in ("x", "y", "yag", "xag"))
    + ("wb_y", "wb_x", "wb_xag", "wb_yag", "right_core", "norm")
)


def dot(a, b, contract=((1,), (0,))):
    return lax.dot_general(
        a, b, (contract, ((), ())), precision=HIGHEST, preferred_element_type=jnp.float32
    )


def split(v):
    high = v.astype(jnp.bfloat16)
    return high, (v - high.astype(jnp.float32)).astype(jnp.bfloat16)


def dot3(a, b):
    a_high, a_low = split(a)
    b_high, b_low = split(b)

    def one(u, v):
        return lax.dot_general(u, v, (((1,), (0,)), ((), ())), preferred_element_type=jnp.float32)

    return one(a_high, b_high) + (one(a_high, b_low) + one(a_low, b_high))


def invert_cholesky_block(work):
    b = BLOCK
    groups = b // 8
    lanes = 2 * b
    rows8 = lax.broadcasted_iota(jnp.int32, (8, lanes), 0)
    a = [work[8 * g : 8 * g + 8, :] for g in range(groups)]
    pivots = [jnp.ones((8, lanes), jnp.float32) for _ in range(groups)]

    def spread(k):
        return {g: jnp.broadcast_to(a[g][:, k : k + 1], (8, lanes)) for g in range(k // 8, groups)}

    def sub(v, s):
        return jnp.broadcast_to(v[s : s + 1, :], (8, lanes))

    window = {k: spread(k) for k in range(WINDOW)}
    for j in range(b):
        gj, sj = divmod(j, 8)
        col = window.pop(j)
        pivot = sub(col[gj], sj)
        pivots[gj] = jnp.where(rows8 == sj, pivot, pivots[gj])
        if j == b - 1:
            break
        inv = 1.0 / pivot
        factor = {g: col[g] * inv for g in range((j + 1) // 8, groups)}
        for k in range(j + 1, min(j + WINDOW, b)):
            ahead = sub(col[k // 8], k % 8)
            for g in range(k // 8, groups):
                window[k][g] = window[k][g] - factor[g] * ahead
        row = sub(a[gj], sj)
        for g in range((j + 1) // 8, groups):
            f = factor[g]
            if g == gj:
                f = jnp.where(rows8 > sj, f, 0.0)
            a[g] = a[g] - f * row
        if j + WINDOW < b:
            window[j + WINDOW] = spread(j + WINDOW)
    out = [a[g] * lax.rsqrt(pivots[g]) for g in range(groups)]
    return jnp.concatenate(out, axis=0)[:, b:]


class Plan:
    def __init__(self, nx, ny, nz, rows, cols, rank):
        self.nx, self.ny, self.nz = nx, ny, nz
        self.rows, self.cols, self.rank = rows, cols, rank
        self.half = rank // 2
        self.hcols = cols // 2
        self.piece = rows // nz
        self.gpiece = self.half // ny
        self.chunk = rank // (A_CHUNKS + 1)
        self.ax = self.chunk // nx
        self.ay_rows = max(8, self.ax // ny)
        self.ay_split = ny * self.ay_rows // self.ax
        self.ay_cols = self.hcols // self.ay_split
        self.by = self.chunk // ny
        self.bx_rows = max(8, self.by // nx)
        self.bx_split = nx * self.bx_rows // self.by
        self.bx_cols = self.hcols // self.bx_split


def kernel(
    p,
    m_hbm,
    q_hbm,
    new_out,
    right_out,
    left_out,
    m_ref,
    q_ref,
    part,
    left_in,
    left,
    gram_part,
    gram_core,
    gram_half,
    gram_y,
    gram_x,
    gram,
    work,
    w_part,
    w_core,
    w_half,
    wa_in,
    wa_sum,
    wa_piece_in,
    wb_in,
    wb_sum,
    wb_piece_in,
    w_full,
    inverse_ref,
    right,
    norm_in,
    norm_out,
    send,
    recv,
    local,
):
    nx, ny, nz, rank = p.nx, p.ny, p.nz, p.rank
    half, hcols, piece, gpiece = p.half, p.hcols, p.piece, p.gpiece
    row_at = lax.axis_index("row")
    z = lax.axis_index("col")
    c = row_at % CORES
    y = (row_at // CORES) % ny
    x = row_at // (CORES * ny)
    other_row = (x * ny + y) * CORES + (1 - c)
    other = {"row": other_row}

    def at_z(t):
        return {"col": t}

    def at_z_other(t):
        return {"row": other_row, "col": t}

    def at_y(t):
        return {"row": (x * ny + t) * CORES + c}

    def at_x(t):
        return {"row": (t * ny + y) * CORES + c}

    def push(stage, src, dst, target):
        s = STAGES.index(stage)
        pltpu.make_async_remote_copy(
            src_ref=src,
            dst_ref=dst,
            send_sem=send.at[s],
            recv_sem=recv.at[s],
            device_id=target,
            device_id_type=MESH,
        ).start()

    def landed(stage, ref):
        pltpu.make_async_copy(ref, ref, recv.at[STAGES.index(stage)]).wait()

    def sent(stage, ref):
        pltpu.make_async_copy(ref, ref, send.at[STAGES.index(stage)]).wait()

    def span(start, size, step=8):
        return pl.ds(pl.multiple_of(start, step), size)

    def rows_of(ref, start, size):
        return ref.at[span(start, size)]

    def far_first(t, n):
        h = t // 2
        return n // 2 + h * (2 * (t % 2) - 1)

    def each(n, fn):
        def body(t, carry):
            fn(far_first(t, n))
            return carry

        lax.fori_loop(1, n, body, 0)

    barrier = pltpu.get_barrier_semaphore()

    def greet(target):
        pl.semaphore_signal(barrier, inc=1, device_id=target, device_id_type=MESH)

    each(nz, lambda t: greet(at_z((z + t) % nz)))
    load_m = pltpu.make_async_copy(m_hbm, m_ref, local.at[0])
    load_q = pltpu.make_async_copy(q_hbm, q_ref, local.at[1])
    load_m.start()
    load_q.start()
    each(ny, lambda t: greet(at_y((y + t) % ny)))
    each(nx, lambda t: greet(at_x((x + t) % nx)))
    each(nz, lambda t: greet(at_z_other((z + t) % nz)))
    greet(other)
    load_m.wait()
    load_q.wait()
    part[...] = dot(m_ref[...], q_ref[...])
    pl.semaphore_wait(barrier, 2 * nz + ny + nx - 3)

    def left_send(t):
        to = (z + t) % nz
        push("left_rs", rows_of(part, to * piece, piece), rows_of(left_in, (t - 1) * piece, piece), at_z(to))

    each(nz, left_send)
    landed("left_rs", left_in)
    total = part[span(z * piece, piece), :]
    for t in range(nz - 1):
        total = total + left_in[t * piece : (t + 1) * piece, :]
    left[span(z * piece, piece), :] = total
    mine = rows_of(left, z * piece, piece)
    each(nz, lambda t: push("left_ag", mine, mine, at_z((z + t) % nz)))
    landed("left_ag", left_in)

    left_now = left[...]
    left_t = work.at[:, 0 : p.rows]
    left_t[...] = left_now.T
    gram_part[...] = dot(left_t[...], left_now)
    push("gram_core", rows_of(gram_part, (1 - c) * half, half), gram_core, other)
    w_part[...] = dot3(left_t[...], m_ref[:, span((1 - c) * hcols, hcols, 128)])
    push("w_core", w_part, w_core, other)
    landed("gram_core", gram_core)
    gram_half[...] = gram_part[span(c * half, half), :] + gram_core[...]

    def gram_y_send(t):
        to = (y + t) % ny
        push("gram_y", rows_of(gram_half, to * gpiece, gpiece), rows_of(gram_y, (t - 1) * gpiece, gpiece), at_y(to))

    each(ny, gram_y_send)
    w_half[...] = dot3(left_t[...], m_ref[:, span(c * hcols, hcols, 128)])
    landed("w_core", w_core)
    w_half[...] = w_half[...] + w_core[...]
    base_b = A_CHUNKS * p.chunk

    def a_piece(ref, base, k):
        return ref.at[
            span(base + (k // p.ay_split) * p.ay_rows, p.ay_rows),
            span((k % p.ay_split) * p.ay_cols, p.ay_cols, 128),
        ]

    def b_piece(ref, base, k):
        return ref.at[
            span(base + (k // p.bx_split) * p.bx_rows, p.bx_rows),
            span((k % p.bx_split) * p.bx_cols, p.bx_cols, 128),
        ]

    def a_start(i):
        def send_x(t):
            to = (x + t) % nx
            push(
                f"wa{i}_x",
                rows_of(w_half, i * p.chunk + to * p.ax, p.ax),
                rows_of(wa_in.at[i], (t - 1) * p.ax, p.ax),
                at_x(to),
            )

        each(nx, send_x)

    def b_start():
        def send_y(t):
            to = (y + t) % ny
            push("wb_y", rows_of(w_half, base_b + to * p.by, p.by), rows_of(wb_in, (t - 1) * p.by, p.by), at_y(to))

        each(ny, send_y)

    def a_second(i):
        def send_y(t):
            to = (y + t) % ny
            push(
                f"wa{i}_y",
                a_piece(wa_sum.at[i], 0, to),
                rows_of(wa_piece_in.at[i], (t - 1) * p.ay_rows, p.ay_rows),
                at_y(to),
            )

        landed(f"wa{i}_x", wa_in.at[i])
        total = w_half[span(i * p.chunk + x * p.ax, p.ax), :]
        for t in range(nx - 1):
            total = total + wa_in[i, t * p.ax : (t + 1) * p.ax, :]
        wa_sum[i] = total
        each(ny, send_y)

    def b_second():
        def send_x(t):
            to = (x + t) % nx
            push("wb_x", b_piece(wb_sum, 0, to), rows_of(wb_piece_in, (t - 1) * p.bx_rows, p.bx_rows), at_x(to))

        landed("wb_y", wb_in)
        total = w_half[span(base_b + y * p.by, p.by), :]
        for t in range(ny - 1):
            total = total + wb_in[t * p.by : (t + 1) * p.by, :]
        wb_sum[...] = total
        each(nx, send_x)

    def a_gather(i):
        landed(f"wa{i}_y", wa_piece_in.at[i])
        total = a_piece(wa_sum.at[i], 0, y)[...]
        for t in range(ny - 1):
            total = total + wa_piece_in[i, t * p.ay_rows : (t + 1) * p.ay_rows, :]
        mine_w = a_piece(w_full, i * p.chunk + x * p.ax, y)
        mine_w[...] = total
        each(ny, lambda t: push(f"wa{i}_yag", mine_w, mine_w, at_y((y + t) % ny)))

    def b_gather():
        landed("wb_x", wb_piece_in)
        total = b_piece(wb_sum, 0, x)[...]
        for t in range(nx - 1):
            total = total + wb_piece_in[t * p.bx_rows : (t + 1) * p.bx_rows, :]
        mine_b = b_piece(w_full, base_b + y * p.by, x)
        mine_b[...] = total
        each(nx, lambda t: push("wb_xag", mine_b, mine_b, at_x((x + t) % nx)))

    def a_last(i):
        landed(f"wa{i}_yag", wa_piece_in.at[i])
        rows_a = rows_of(w_full, i * p.chunk + x * p.ax, p.ax)
        each(nx, lambda t: push(f"wa{i}_xag", rows_a, rows_a, at_x((x + t) % nx)))

    def b_last():
        landed("wb_xag", wb_piece_in)
        rows_b = rows_of(w_full, base_b + y * p.by, p.by)
        each(ny, lambda t: push("wb_yag", rows_b, rows_b, at_y((y + t) % ny)))

    for i in range(A_CHUNKS):
        a_start(i)
    b_start()
    a_second(0)
    landed("gram_y", gram_y)
    total = gram_half[span(y * gpiece, gpiece), :]
    for t in range(ny - 1):
        total = total + gram_y[t * gpiece : (t + 1) * gpiece, :]
    gram_x[span(x * gpiece, gpiece), :] = total
    mine_g = rows_of(gram_x, x * gpiece, gpiece)
    each(nx, lambda t: push("gram_x", mine_g, mine_g, at_x((x + t) % nx)))
    for i in range(1, A_CHUNKS):
        a_second(i)
    b_second()
    landed("gram_x", gram_x.at[pl.ds(0, (nx - 1) * gpiece)])
    total = gram_x[0:gpiece, :]
    for t in range(1, nx):
        total = total + gram_x[t * gpiece : (t + 1) * gpiece, :]
    at = c * half + y * gpiece
    gram[span(at, gpiece), :] = total
    mine_a = rows_of(gram, at, gpiece)
    each(ny, lambda t: push("gram_yag", mine_a, mine_a, at_y((y + t) % ny)))
    a_gather(0)
    b_gather()
    for i in range(1, A_CHUNKS):
        a_gather(i)
    b_last()
    landed("gram_yag", gram_y)
    mine_h = rows_of(gram, c * half, half)
    push("gram_cag", mine_h, mine_h, other)
    a_last(0)
    landed("gram_cag", gram_half)

    nb = rank // BLOCK
    work[...] = gram[...]
    eye = (
        lax.broadcasted_iota(jnp.int32, (BLOCK, BLOCK), 0) == lax.broadcasted_iota(jnp.int32, (BLOCK, BLOCK), 1)
    ).astype(jnp.float32)

    def after_block(k):
        if k == 0:
            for i in range(1, A_CHUNKS):
                a_last(i)

    inverse_rows = []
    solved = []
    for k in range(nb):
        lo, hi = k * BLOCK, (k + 1) * BLOCK
        diag = work[lo:hi, lo:hi]
        inv_kk = invert_cholesky_block(jnp.concatenate([diag, eye], axis=1))
        if hi < rank:
            u = dot(inv_kk, work[lo:hi, hi:])
            solved.append(u)
            work[hi:, hi:] = work[hi:, hi:] - dot(u, u, ((0,), (0,)))
        inv_row = inv_kk
        if k > 0:
            acc = None
            for i in range(k):
                term = dot(solved[i][:, lo - (i + 1) * BLOCK : lo - i * BLOCK], inverse_rows[i], ((0,), (0,)))
                width = (i + 1) * BLOCK
                if width < lo:
                    term = jnp.concatenate([term, jnp.zeros((BLOCK, lo - width), jnp.float32)], axis=1)
                acc = term if acc is None else acc + term
            inv_row = jnp.concatenate([-dot(inv_kk, acc), inv_kk], axis=1)
        inverse_rows.append(inv_row)
        if hi < rank:
            inv_row = jnp.concatenate([inv_row, jnp.zeros((BLOCK, rank - hi), jnp.float32)], axis=1)
        inverse_ref[lo:hi, :] = inv_row
        after_block(k)
    landed("wb_yag", wb_in)
    for i in range(A_CHUNKS):
        landed(f"wa{i}_xag", wa_in.at[i])
    r = dot3(inverse_ref[...], w_full[...])
    right[c] = r
    push("right_core", right.at[c], right.at[c], other)
    folded = r[:, 0:128] * r[:, 0:128]
    for t in range(1, hcols // 128):
        folded = folded + r[:, 128 * t : 128 * (t + 1)] * r[:, 128 * t : 128 * (t + 1)]
    squares = dot(jnp.ones((8, 128), jnp.float32), folded, ((1,), (1,)))
    norm_out[...] = squares[0:1, :]

    def norm_send(t):
        to = (z + t) % nz
        push("norm", norm_out, norm_in.at[t - 1], at_z(to))
        push("norm", norm_out, norm_in.at[nz - 1 + t], at_z_other(to))

    each(nz, norm_send)
    push("norm", norm_out, norm_in.at[nz - 1], other)
    left_orth = dot(left[...], inverse_ref[...], ((1,), (1,)))
    half_orth = 0.5 * left_orth
    mine_cols = span(c * hcols, hcols, 128)
    new_out[:, mine_cols] = m_ref[:, mine_cols] - dot3(half_orth, right[c])
    landed("right_core", w_half)
    other_cols = span((1 - c) * hcols, hcols, 128)
    new_out[:, other_cols] = m_ref[:, other_cols] - dot3(half_orth, right[1 - c])
    right_out[...] = right[...]
    landed("norm", norm_in)
    total = norm_out[...]
    for t in range(2 * nz - 1):
        total = total + norm_in[t]
    scale = math.sqrt(ROWS * COLS / RANK)
    left_out[...] = left_orth * (scale / jnp.sqrt(total + 1e-06))

    sent("left_rs", left_in)
    sent("left_ag", left_in)
    sent("gram_core", gram_core)
    sent("gram_y", gram_y)
    sent("gram_x", gram_x.at[pl.ds(0, (nx - 1) * gpiece)])
    sent("gram_yag", gram_y)
    sent("gram_cag", gram_half)
    sent("w_core", w_core)
    for i in range(A_CHUNKS):
        sent(f"wa{i}_x", wa_in.at[i])
        sent(f"wa{i}_y", wa_piece_in.at[i])
        sent(f"wa{i}_yag", wa_piece_in.at[i])
        sent(f"wa{i}_xag", wa_in.at[i])
    sent("wb_y", wb_in)
    sent("wb_x", wb_piece_in)
    sent("wb_xag", wb_piece_in)
    sent("wb_yag", wb_in)
    sent("right_core", w_half)
    sent("norm", norm_in)


def write_outputs(new_ref, right_ref, left_ref, new_hbm, upd_hbm, upd, sems):
    hcols = right_ref.shape[2]
    copies = [pltpu.make_async_copy(new_ref, new_hbm, sems.at[0])]
    copies[0].start()
    for h in range(2):
        at = pl.ds(h * hcols, hcols)
        upd[:, at] = dot3(left_ref[...], right_ref[h])
        copies.append(pltpu.make_async_copy(upd.at[:, at], upd_hbm.at[:, at], sems.at[1 + h]))
        copies[-1].start()
    for copy in copies:
        copy.wait()


def local_step(p, momentum, right_factor):
    f32 = jnp.float32
    vmem = lambda *shape: pltpu.VMEM(shape, f32)
    shaped = lambda *shape: jax.ShapeDtypeStruct(shape, f32)
    any_spec = pl.BlockSpec(memory_space=pl.ANY)
    hbm_spec = pl.BlockSpec(memory_space=pltpu.HBM)
    vmem_spec = pl.BlockSpec(memory_space=pltpu.VMEM)
    new, right, left = pl.pallas_call(
        functools.partial(kernel, p),
        out_shape=(shaped(p.rows, p.cols), shaped(2, p.rank, p.hcols), shaped(p.rows, p.rank)),
        in_specs=[hbm_spec, hbm_spec],
        out_specs=(vmem_spec,) * 3,
        scratch_shapes=[
            vmem(p.rows, p.cols),
            vmem(p.cols, p.rank),
            vmem(p.rows, p.rank),
            vmem(p.rows - p.piece, p.rank),
            vmem(p.rows, p.rank),
            vmem(p.rank, p.rank),
            vmem(p.half, p.rank),
            vmem(p.half, p.rank),
            vmem(p.half - p.gpiece, p.rank),
            vmem(p.nx * p.gpiece, p.rank),
            vmem(p.rank, p.rank),
            vmem(p.rank, p.rank),
            vmem(p.rank, p.hcols),
            vmem(p.rank, p.hcols),
            vmem(p.rank, p.hcols),
            vmem(A_CHUNKS, p.chunk - p.ax, p.hcols),
            vmem(A_CHUNKS, p.ax, p.hcols),
            vmem(A_CHUNKS, (p.ny - 1) * p.ay_rows, p.ay_cols),
            vmem(p.chunk - p.by, p.hcols),
            vmem(p.by, p.hcols),
            vmem((p.nx - 1) * p.bx_rows, p.bx_cols),
            vmem(p.rank, p.hcols),
            vmem(p.rank, p.rank),
            vmem(2, p.rank, p.hcols),
            vmem(2 * p.nz - 1, 1, p.rank),
            vmem(1, p.rank),
            pltpu.SemaphoreType.DMA((len(STAGES),)),
            pltpu.SemaphoreType.DMA((len(STAGES),)),
            pltpu.SemaphoreType.DMA((2,)),
        ],
        compiler_params=pltpu.CompilerParams(collective_id=0, has_side_effects=True, vmem_limit_bytes=VMEM_BYTES),
        name="dion",
    )(
        pltpu.with_memory_space_constraint(momentum, pltpu.HBM),
        pltpu.with_memory_space_constraint(right_factor, pltpu.HBM),
    )
    return pl.pallas_call(
        write_outputs,
        out_shape=(shaped(p.rows, p.cols),) * 2,
        in_specs=[vmem_spec] * 3,
        out_specs=(any_spec, any_spec),
        scratch_shapes=[vmem(p.rows, p.cols), pltpu.SemaphoreType.DMA((3,))],
        compiler_params=pltpu.CompilerParams(vmem_limit_bytes=8 * 2**20),
        name="outputs",
    )(new, right, left)


def solution(mesh):
    nz = mesh.shape["col"]
    ny = Y_CHIPS
    nx = mesh.shape["row"] // (ny * CORES)

    def local(momentum, right_factor):
        plan = Plan(nx, ny, nz, momentum.shape[0], momentum.shape[1], right_factor.shape[1])
        return local_step(plan, momentum, right_factor)

    in_specs = (P("row", "col"), P("col", None))
    out_specs = (P("row", "col"), P("row", "col"))
    return jax.shard_map(local, mesh=mesh, in_specs=in_specs, out_specs=out_specs, check_vma=False)
```

```python
import functools
import math

import jax
import jax.numpy as jnp
from jax import lax
from jax.experimental import pallas as pl
from jax.experimental.pallas import tpu as pltpu
from jax.sharding import PartitionSpec as P

ROWS = 8192
COLS = 16384
RANK = 256
CORES = 2
Y_CHIPS = 8
BLOCK = 64
WINDOW = 8
VMEM_BYTES = 24 * 2**20
HIGHEST = lax.Precision.HIGHEST
MESH = pl.DeviceIdType.MESH

A_CHUNKS = 3
STAGES = (
    ("left_rs", "left_ag", "m_core", "left_core", "gram_y", "gram_x", "gram_yag", "gram_cag")
    + tuple(f"wa{i}_{s}" for i in range(A_CHUNKS) for s in ("x", "y", "yag", "xag"))
    + ("wb_y", "wb_x", "wb_xag", "wb_yag", "right_core", "norm")
)


def dot(a, b, contract=((1,), (0,))):
    return lax.dot_general(
        a, b, (contract, ((), ())), precision=HIGHEST, preferred_element_type=jnp.float32
    )


def split(v):
    high = v.astype(jnp.bfloat16)
    return high, (v - high.astype(jnp.float32)).astype(jnp.bfloat16)


def dot3(a, b):
    a_high, a_low = split(a)
    b_high, b_low = split(b)

    def one(u, v):
        return lax.dot_general(u, v, (((1,), (0,)), ((), ())), preferred_element_type=jnp.float32)

    return one(a_high, b_high) + (one(a_high, b_low) + one(a_low, b_high))


def invert_cholesky_block(work):
    b = BLOCK
    groups = b // 8
    lanes = 2 * b
    rows8 = lax.broadcasted_iota(jnp.int32, (8, lanes), 0)
    a = [work[8 * g : 8 * g + 8, :] for g in range(groups)]
    pivots = [jnp.ones((8, lanes), jnp.float32) for _ in range(groups)]

    def spread(k):
        return {g: jnp.broadcast_to(a[g][:, k : k + 1], (8, lanes)) for g in range(k // 8, groups)}

    def sub(v, s):
        return jnp.broadcast_to(v[s : s + 1, :], (8, lanes))

    window = {k: spread(k) for k in range(WINDOW)}
    for j in range(b):
        gj, sj = divmod(j, 8)
        col = window.pop(j)
        pivot = sub(col[gj], sj)
        pivots[gj] = jnp.where(rows8 == sj, pivot, pivots[gj])
        if j == b - 1:
            break
        inv = 1.0 / pivot
        factor = {g: col[g] * inv for g in range((j + 1) // 8, groups)}
        for k in range(j + 1, min(j + WINDOW, b)):
            ahead = sub(col[k // 8], k % 8)
            for g in range(k // 8, groups):
                window[k][g] = window[k][g] - factor[g] * ahead
        row = sub(a[gj], sj)
        for g in range((j + 1) // 8, groups):
            f = factor[g]
            if g == gj:
                f = jnp.where(rows8 > sj, f, 0.0)
            a[g] = a[g] - f * row
        if j + WINDOW < b:
            window[j + WINDOW] = spread(j + WINDOW)
    out = [a[g] * lax.rsqrt(pivots[g]) for g in range(groups)]
    return jnp.concatenate(out, axis=0)[:, b:]


class Plan:
    def __init__(self, nx, ny, nz, rows, cols, rank):
        self.nx, self.ny, self.nz = nx, ny, nz
        self.rows, self.cols, self.rank = rows, cols, rank
        self.half = rank // 2
        self.hcols = cols // 2
        self.piece = rows // nz
        self.ghalf = 3 * self.half // 2
        self.gpiece = self.ghalf // ny
        self.chunk = rank // (A_CHUNKS + 1)
        self.ax = self.chunk // nx
        self.ay_rows = max(8, self.ax // ny)
        self.ay_split = ny * self.ay_rows // self.ax
        self.ay_cols = self.hcols // self.ay_split
        self.by = self.chunk // ny
        self.bx_rows = max(8, self.by // nx)
        self.bx_split = nx * self.bx_rows // self.by
        self.bx_cols = self.hcols // self.bx_split


def kernel(
    p,
    m_hbm,
    q_hbm,
    new_out,
    right_out,
    left_out,
    m_ref,
    q_ref,
    part,
    left_in,
    left,
    left_other,
    m_other,
    gram_part,
    gram_y,
    gram_x,
    gram,
    work,
    w_half,
    wa_in,
    wa_sum,
    wa_piece_in,
    wb_in,
    wb_sum,
    wb_piece_in,
    w_full,
    inverse_ref,
    right,
    norm_in,
    norm_out,
    send,
    recv,
    local,
):
    nx, ny, nz, rank = p.nx, p.ny, p.nz, p.rank
    half, hcols, piece, ghalf, gpiece = p.half, p.hcols, p.piece, p.ghalf, p.gpiece
    row_at = lax.axis_index("row")
    z = lax.axis_index("col")
    c = row_at % CORES
    y = (row_at // CORES) % ny
    x = row_at // (CORES * ny)
    other_row = (x * ny + y) * CORES + (1 - c)
    other = {"row": other_row}

    def at_z(t):
        return {"col": t}

    def at_z_other(t):
        return {"row": other_row, "col": t}

    def at_y(t):
        return {"row": (x * ny + t) * CORES + c}

    def at_x(t):
        return {"row": (t * ny + y) * CORES + c}

    def push(stage, src, dst, target):
        s = STAGES.index(stage)
        pltpu.make_async_remote_copy(
            src_ref=src,
            dst_ref=dst,
            send_sem=send.at[s],
            recv_sem=recv.at[s],
            device_id=target,
            device_id_type=MESH,
        ).start()

    def landed(stage, ref):
        pltpu.make_async_copy(ref, ref, recv.at[STAGES.index(stage)]).wait()

    def sent(stage, ref):
        pltpu.make_async_copy(ref, ref, send.at[STAGES.index(stage)]).wait()

    def span(start, size, step=8):
        return pl.ds(pl.multiple_of(start, step), size)

    def rows_of(ref, start, size):
        return ref.at[span(start, size)]

    def far_first(t, n):
        h = t // 2
        return n // 2 + h * (2 * (t % 2) - 1)

    def each(n, fn):
        def body(t, carry):
            fn(far_first(t, n))
            return carry

        lax.fori_loop(1, n, body, 0)

    barrier = pltpu.get_barrier_semaphore()

    def greet(target):
        pl.semaphore_signal(barrier, inc=1, device_id=target, device_id_type=MESH)

    def greet_z(t):
        greet(at_z((z + t) % nz))
        greet(at_z_other((z + t) % nz))

    each(nz, greet_z)
    load_m = pltpu.make_async_copy(m_hbm, m_ref, local.at[0])
    load_q = pltpu.make_async_copy(q_hbm, q_ref, local.at[1])
    load_m.start()
    load_q.start()
    each(ny, lambda t: greet(at_y((y + t) % ny)))
    each(nx, lambda t: greet(at_x((x + t) % nx)))
    greet(other)
    load_m.wait()
    load_q.wait()
    part[...] = dot(m_ref[...], q_ref[...])
    pl.semaphore_wait(barrier, 2 * nz + ny + nx - 3)

    def left_send(t):
        to = (z + t) % nz
        push("left_rs", rows_of(part, to * piece, piece), rows_of(left_in, (t - 1) * piece, piece), at_z(to))

    each(nz, left_send)
    mine_cols = span(c * hcols, hcols, 128)
    other_cols = span((1 - c) * hcols, hcols, 128)
    push("m_core", m_ref.at[:, other_cols], m_other, other)
    landed("left_rs", left_in)
    total = part[span(z * piece, piece), :]
    for t in range(nz - 1):
        total = total + left_in[t * piece : (t + 1) * piece, :]
    left[span(z * piece, piece), :] = total
    mine = rows_of(left, z * piece, piece)
    each(nz, lambda t: push("left_ag", mine, mine, at_z((z + t) % nz)))
    landed("left_ag", left_in)

    push("left_core", left, left_other, other)
    left_now = left[...]
    left_t = left_now.T
    gram_own = dot(left_t, left_now)
    w_half[...] = dot3(left_t, m_ref[:, mine_cols])
    landed("left_core", left_other)
    left_now = left_other[...]
    left_t = left_now.T
    gram_pair = gram_own + dot(left_t, left_now)
    gram_part[0:half, :] = gram_pair[0:half, 0:half]
    gram_part[half : 2 * half, :] = gram_pair[0:half, half:]
    gram_part[2 * half :, :] = gram_pair[half:, half:]

    def gram_y_send(t):
        to = (y + t) % ny
        push(
            "gram_y",
            rows_of(gram_part, c * ghalf + to * gpiece, gpiece),
            rows_of(gram_y, (t - 1) * gpiece, gpiece),
            at_y(to),
        )

    each(ny, gram_y_send)
    landed("m_core", m_other)
    w_half[...] = w_half[...] + dot3(left_t, m_other[...])
    base_b = A_CHUNKS * p.chunk

    def a_piece(ref, base, k):
        return ref.at[
            span(base + (k // p.ay_split) * p.ay_rows, p.ay_rows),
            span((k % p.ay_split) * p.ay_cols, p.ay_cols, 128),
        ]

    def b_piece(ref, base, k):
        return ref.at[
            span(base + (k // p.bx_split) * p.bx_rows, p.bx_rows),
            span((k % p.bx_split) * p.bx_cols, p.bx_cols, 128),
        ]

    def a_start(i):
        def send_x(t):
            to = (x + t) % nx
            push(
                f"wa{i}_x",
                rows_of(w_half, i * p.chunk + to * p.ax, p.ax),
                rows_of(wa_in.at[i], (t - 1) * p.ax, p.ax),
                at_x(to),
            )

        each(nx, send_x)

    def b_start():
        def send_y(t):
            to = (y + t) % ny
            push("wb_y", rows_of(w_half, base_b + to * p.by, p.by), rows_of(wb_in, (t - 1) * p.by, p.by), at_y(to))

        each(ny, send_y)

    def a_second(i):
        def send_y(t):
            to = (y + t) % ny
            push(
                f"wa{i}_y",
                a_piece(wa_sum.at[i], 0, to),
                rows_of(wa_piece_in.at[i], (t - 1) * p.ay_rows, p.ay_rows),
                at_y(to),
            )

        landed(f"wa{i}_x", wa_in.at[i])
        total = w_half[span(i * p.chunk + x * p.ax, p.ax), :]
        for t in range(nx - 1):
            total = total + wa_in[i, t * p.ax : (t + 1) * p.ax, :]
        wa_sum[i] = total
        each(ny, send_y)

    def b_second():
        def send_x(t):
            to = (x + t) % nx
            push("wb_x", b_piece(wb_sum, 0, to), rows_of(wb_piece_in, (t - 1) * p.bx_rows, p.bx_rows), at_x(to))

        landed("wb_y", wb_in)
        total = w_half[span(base_b + y * p.by, p.by), :]
        for t in range(ny - 1):
            total = total + wb_in[t * p.by : (t + 1) * p.by, :]
        wb_sum[...] = total
        each(nx, send_x)

    def a_gather(i):
        landed(f"wa{i}_y", wa_piece_in.at[i])
        total = a_piece(wa_sum.at[i], 0, y)[...]
        for t in range(ny - 1):
            total = total + wa_piece_in[i, t * p.ay_rows : (t + 1) * p.ay_rows, :]
        mine_w = a_piece(w_full, i * p.chunk + x * p.ax, y)
        mine_w[...] = total
        each(ny, lambda t: push(f"wa{i}_yag", mine_w, mine_w, at_y((y + t) % ny)))

    def b_gather():
        landed("wb_x", wb_piece_in)
        total = b_piece(wb_sum, 0, x)[...]
        for t in range(nx - 1):
            total = total + wb_piece_in[t * p.bx_rows : (t + 1) * p.bx_rows, :]
        mine_b = b_piece(w_full, base_b + y * p.by, x)
        mine_b[...] = total
        each(nx, lambda t: push("wb_xag", mine_b, mine_b, at_x((x + t) % nx)))

    def a_last(i):
        landed(f"wa{i}_yag", wa_piece_in.at[i])
        rows_a = rows_of(w_full, i * p.chunk + x * p.ax, p.ax)
        each(nx, lambda t: push(f"wa{i}_xag", rows_a, rows_a, at_x((x + t) % nx)))

    def b_last():
        landed("wb_xag", wb_piece_in)
        rows_b = rows_of(w_full, base_b + y * p.by, p.by)
        each(ny, lambda t: push("wb_yag", rows_b, rows_b, at_y((y + t) % ny)))

    for i in range(A_CHUNKS):
        a_start(i)
    b_start()
    a_second(0)
    landed("gram_y", gram_y)
    total = gram_part[span(c * ghalf + y * gpiece, gpiece), :]
    for t in range(ny - 1):
        total = total + gram_y[t * gpiece : (t + 1) * gpiece, :]
    gram_x[span(x * gpiece, gpiece), :] = total
    mine_g = rows_of(gram_x, x * gpiece, gpiece)
    each(nx, lambda t: push("gram_x", mine_g, mine_g, at_x((x + t) % nx)))
    for i in range(1, A_CHUNKS):
        a_second(i)
    b_second()
    landed("gram_x", gram_x.at[pl.ds(0, (nx - 1) * gpiece)])
    total = gram_x[0:gpiece, :]
    for t in range(1, nx):
        total = total + gram_x[t * gpiece : (t + 1) * gpiece, :]
    at = c * ghalf + y * gpiece
    gram[span(at, gpiece), :] = total
    mine_a = rows_of(gram, at, gpiece)
    each(ny, lambda t: push("gram_yag", mine_a, mine_a, at_y((y + t) % ny)))
    a_gather(0)
    b_gather()
    for i in range(1, A_CHUNKS):
        a_gather(i)
    landed("gram_yag", gram_y)
    mine_h = rows_of(gram, c * ghalf, ghalf)
    push("gram_cag", mine_h, mine_h, other)
    b_last()
    a_last(0)
    landed("gram_cag", mine_h)

    nb = rank // BLOCK
    work[0:half, 0:half] = gram[0:half, :]
    work[0:half, half:] = gram[half : 2 * half, :]
    work[half:, 0:half] = jnp.zeros((half, half), jnp.float32)
    work[half:, half:] = gram[2 * half :, :]
    eye = (
        lax.broadcasted_iota(jnp.int32, (BLOCK, BLOCK), 0) == lax.broadcasted_iota(jnp.int32, (BLOCK, BLOCK), 1)
    ).astype(jnp.float32)

    def after_block(k):
        if k + 1 < A_CHUNKS:
            a_last(k + 1)

    inverse_rows = []
    solved = []
    for k in range(nb):
        lo, hi = k * BLOCK, (k + 1) * BLOCK
        diag = work[lo:hi, lo:hi]
        inv_kk = invert_cholesky_block(jnp.concatenate([diag, eye], axis=1))
        if hi < rank:
            u = dot(inv_kk, work[lo:hi, hi:])
            solved.append(u)
            work[hi:, hi:] = work[hi:, hi:] - dot(u, u, ((0,), (0,)))
        inv_row = inv_kk
        if k > 0:
            acc = None
            for i in range(k):
                term = dot(solved[i][:, lo - (i + 1) * BLOCK : lo - i * BLOCK], inverse_rows[i], ((0,), (0,)))
                width = (i + 1) * BLOCK
                if width < lo:
                    term = jnp.concatenate([term, jnp.zeros((BLOCK, lo - width), jnp.float32)], axis=1)
                acc = term if acc is None else acc + term
            inv_row = jnp.concatenate([-dot(inv_kk, acc), inv_kk], axis=1)
        inverse_rows.append(inv_row)
        if hi < rank:
            inv_row = jnp.concatenate([inv_row, jnp.zeros((BLOCK, rank - hi), jnp.float32)], axis=1)
        inverse_ref[lo:hi, :] = inv_row
        after_block(k)
    landed("wb_yag", wb_in)
    for i in range(A_CHUNKS):
        landed(f"wa{i}_xag", wa_in.at[i])
    r = dot3(inverse_ref[...], w_full[...])
    right[c] = r
    push("right_core", right.at[c], right.at[c], other)
    folded = r[:, 0:128] * r[:, 0:128]
    for t in range(1, hcols // 128):
        folded = folded + r[:, 128 * t : 128 * (t + 1)] * r[:, 128 * t : 128 * (t + 1)]
    squares = dot(jnp.ones((8, 128), jnp.float32), folded, ((1,), (1,)))
    norm_out[...] = squares[0:1, :]

    def norm_send(t):
        to = (z + t) % nz
        push("norm", norm_out, norm_in.at[t - 1], at_z(to))
        push("norm", norm_out, norm_in.at[nz - 1 + t], at_z_other(to))

    each(nz, norm_send)
    push("norm", norm_out, norm_in.at[nz - 1], other)
    left_orth = dot(left[...], inverse_ref[...], ((1,), (1,)))
    half_orth = 0.5 * left_orth
    new_out[:, mine_cols] = m_ref[:, mine_cols] - dot3(half_orth, right[c])
    landed("right_core", w_half)
    new_out[:, other_cols] = m_ref[:, other_cols] - dot3(half_orth, right[1 - c])
    right_out[...] = right[...]
    landed("norm", norm_in)
    total = norm_out[...]
    for t in range(2 * nz - 1):
        total = total + norm_in[t]
    scale = math.sqrt(ROWS * COLS / RANK)
    left_out[...] = left_orth * (scale / jnp.sqrt(total + 1e-06))

    sent("left_rs", left_in)
    sent("left_ag", left_in)
    sent("m_core", m_other)
    sent("left_core", left_other)
    sent("gram_y", gram_y)
    sent("gram_x", gram_x.at[pl.ds(0, (nx - 1) * gpiece)])
    sent("gram_yag", gram_y)
    sent("gram_cag", mine_h)
    for i in range(A_CHUNKS):
        sent(f"wa{i}_x", wa_in.at[i])
        sent(f"wa{i}_y", wa_piece_in.at[i])
        sent(f"wa{i}_yag", wa_piece_in.at[i])
        sent(f"wa{i}_xag", wa_in.at[i])
    sent("wb_y", wb_in)
    sent("wb_x", wb_piece_in)
    sent("wb_xag", wb_piece_in)
    sent("wb_yag", wb_in)
    sent("right_core", w_half)
    sent("norm", norm_in)


def write_outputs(new_ref, right_ref, left_ref, new_hbm, upd_hbm, upd, sems):
    hcols = right_ref.shape[2]
    copies = [pltpu.make_async_copy(new_ref, new_hbm, sems.at[0])]
    copies[0].start()
    for h in range(2):
        at = pl.ds(h * hcols, hcols)
        upd[:, at] = dot3(left_ref[...], right_ref[h])
        copies.append(pltpu.make_async_copy(upd.at[:, at], upd_hbm.at[:, at], sems.at[1 + h]))
        copies[-1].start()
    for copy in copies:
        copy.wait()


def local_step(p, momentum, right_factor):
    f32 = jnp.float32
    vmem = lambda *shape: pltpu.VMEM(shape, f32)
    shaped = lambda *shape: jax.ShapeDtypeStruct(shape, f32)
    any_spec = pl.BlockSpec(memory_space=pl.ANY)
    hbm_spec = pl.BlockSpec(memory_space=pltpu.HBM)
    vmem_spec = pl.BlockSpec(memory_space=pltpu.VMEM)
    new, right, left = pl.pallas_call(
        functools.partial(kernel, p),
        out_shape=(shaped(p.rows, p.cols), shaped(2, p.rank, p.hcols), shaped(p.rows, p.rank)),
        in_specs=[hbm_spec, hbm_spec],
        out_specs=(vmem_spec,) * 3,
        scratch_shapes=[
            vmem(p.rows, p.cols),
            vmem(p.cols, p.rank),
            vmem(p.rows, p.rank),
            vmem(p.rows - p.piece, p.rank),
            vmem(p.rows, p.rank),
            vmem(p.rows, p.rank),
            vmem(p.rows, p.hcols),
            vmem(2 * p.ghalf, p.half),
            vmem(p.ghalf - p.gpiece, p.half),
            vmem(p.nx * p.gpiece, p.half),
            vmem(2 * p.ghalf, p.half),
            vmem(p.rank, p.rank),
            vmem(p.rank, p.hcols),
            vmem(A_CHUNKS, p.chunk - p.ax, p.hcols),
            vmem(A_CHUNKS, p.ax, p.hcols),
            vmem(A_CHUNKS, (p.ny - 1) * p.ay_rows, p.ay_cols),
            vmem(p.chunk - p.by, p.hcols),
            vmem(p.by, p.hcols),
            vmem((p.nx - 1) * p.bx_rows, p.bx_cols),
            vmem(p.rank, p.hcols),
            vmem(p.rank, p.rank),
            vmem(2, p.rank, p.hcols),
            vmem(2 * p.nz - 1, 1, p.rank),
            vmem(1, p.rank),
            pltpu.SemaphoreType.DMA((len(STAGES),)),
            pltpu.SemaphoreType.DMA((len(STAGES),)),
            pltpu.SemaphoreType.DMA((2,)),
        ],
        compiler_params=pltpu.CompilerParams(collective_id=0, has_side_effects=True, vmem_limit_bytes=VMEM_BYTES),
        name="dion",
    )(
        pltpu.with_memory_space_constraint(momentum, pltpu.HBM),
        pltpu.with_memory_space_constraint(right_factor, pltpu.HBM),
    )
    return pl.pallas_call(
        write_outputs,
        out_shape=(shaped(p.rows, p.cols),) * 2,
        in_specs=[vmem_spec] * 3,
        out_specs=(any_spec, any_spec),
        scratch_shapes=[vmem(p.rows, p.cols), pltpu.SemaphoreType.DMA((3,))],
        compiler_params=pltpu.CompilerParams(vmem_limit_bytes=8 * 2**20),
        name="outputs",
    )(new, right, left)


def solution(mesh):
    nz = mesh.shape["col"]
    ny = Y_CHIPS
    nx = mesh.shape["row"] // (ny * CORES)

    def local(momentum, right_factor):
        plan = Plan(nx, ny, nz, momentum.shape[0], momentum.shape[1], right_factor.shape[1])
        return local_step(plan, momentum, right_factor)

    in_specs = (P("row", "col"), P("col", None))
    out_specs = (P("row", "col"), P("row", "col"))
    return jax.shard_map(local, mesh=mesh, in_specs=in_specs, out_specs=out_specs, check_vma=False)
```

```python
import functools
import math

import jax
import jax.numpy as jnp
from jax import lax
from jax.experimental import pallas as pl
from jax.experimental.pallas import tpu as pltpu
from jax.sharding import PartitionSpec as P

ROWS = 8192
COLS = 16384
RANK = 256
CORES = 2
Y_CHIPS = 8
BLOCK = 64
WINDOW = 8
VMEM_BYTES = 24 * 2**20
HIGHEST = lax.Precision.HIGHEST
MESH = pl.DeviceIdType.MESH

A_CHUNKS = 3
STAGES = (
    ("left_rs", "left_ag", "m_core", "left_core", "gram_y", "gram_x", "gram_yag", "gram_cag")
    + tuple(f"wa{i}_{s}" for i in range(A_CHUNKS) for s in ("x", "y", "yag", "xag"))
    + ("wb_y", "wb_x", "wb_xag", "wb_yag", "right_core", "norm")
)


def dot(a, b, contract=((1,), (0,))):
    return lax.dot_general(
        a, b, (contract, ((), ())), precision=HIGHEST, preferred_element_type=jnp.float32
    )


def split(v):
    high = v.astype(jnp.bfloat16)
    return high, (v - high.astype(jnp.float32)).astype(jnp.bfloat16)


def dot3(a, b):
    a_high, a_low = split(a)
    b_high, b_low = split(b)

    def one(u, v):
        return lax.dot_general(u, v, (((1,), (0,)), ((), ())), preferred_element_type=jnp.float32)

    return one(a_high, b_high) + (one(a_high, b_low) + one(a_low, b_high))


def invert_cholesky_block(work):
    b = BLOCK
    groups = b // 8
    lanes = 2 * b
    rows8 = lax.broadcasted_iota(jnp.int32, (8, lanes), 0)
    a = [work[8 * g : 8 * g + 8, :] for g in range(groups)]
    pivots = [jnp.ones((8, lanes), jnp.float32) for _ in range(groups)]

    def spread(k):
        return {g: jnp.broadcast_to(a[g][:, k : k + 1], (8, lanes)) for g in range(k // 8, groups)}

    def sub(v, s):
        return jnp.broadcast_to(v[s : s + 1, :], (8, lanes))

    window = {k: spread(k) for k in range(WINDOW)}
    for j in range(b):
        gj, sj = divmod(j, 8)
        col = window.pop(j)
        pivot = sub(col[gj], sj)
        pivots[gj] = jnp.where(rows8 == sj, pivot, pivots[gj])
        if j == b - 1:
            break
        inv = 1.0 / pivot
        factor = {g: col[g] * inv for g in range((j + 1) // 8, groups)}
        for k in range(j + 1, min(j + WINDOW, b)):
            ahead = sub(col[k // 8], k % 8)
            for g in range(k // 8, groups):
                window[k][g] = window[k][g] - factor[g] * ahead
        row = sub(a[gj], sj)
        for g in range((j + 1) // 8, groups):
            f = factor[g]
            if g == gj:
                f = jnp.where(rows8 > sj, f, 0.0)
            a[g] = a[g] - f * row
        if j + WINDOW < b:
            window[j + WINDOW] = spread(j + WINDOW)
    out = [a[g] * lax.rsqrt(pivots[g]) for g in range(groups)]
    return jnp.concatenate(out, axis=0)[:, b:]


class Plan:
    def __init__(self, nx, ny, nz, rows, cols, rank):
        self.nx, self.ny, self.nz = nx, ny, nz
        self.rows, self.cols, self.rank = rows, cols, rank
        self.half = rank // 2
        self.hcols = cols // 2
        self.piece = rows // nz
        self.ghalf = 3 * self.half // 2
        self.gpiece = self.ghalf // ny
        self.chunk = rank // (A_CHUNKS + 1)
        self.ax = self.chunk // nx
        self.ay_rows = max(8, self.ax // ny)
        self.ay_split = ny * self.ay_rows // self.ax
        self.ay_cols = self.hcols // self.ay_split
        self.by = self.chunk // ny
        self.bx_rows = max(8, self.by // nx)
        self.bx_split = nx * self.bx_rows // self.by
        self.bx_cols = self.hcols // self.bx_split


def kernel(
    p,
    m_hbm,
    q_hbm,
    new_out,
    right_out,
    left_out,
    m_ref,
    q_ref,
    part,
    left_in,
    left,
    left_other,
    m_other,
    gram_part,
    gram_y,
    gram_x,
    gram,
    work,
    w_half,
    wa_in,
    wa_sum,
    wa_piece_in,
    wb_in,
    wb_sum,
    wb_piece_in,
    w_full,
    inverse_ref,
    right,
    norm_in,
    norm_out,
    send,
    recv,
    local,
):
    nx, ny, nz, rank = p.nx, p.ny, p.nz, p.rank
    half, hcols, piece, ghalf, gpiece = p.half, p.hcols, p.piece, p.ghalf, p.gpiece
    row_at = lax.axis_index("row")
    z = lax.axis_index("col")
    c = lax.rem(row_at, CORES)
    y = lax.rem(lax.div(row_at, CORES), ny)
    x = lax.div(row_at, CORES * ny)
    other_row = (x * ny + y) * CORES + (1 - c)
    other = {"row": other_row}

    def at_z(t):
        return {"col": t}

    def at_z_other(t):
        return {"row": other_row, "col": t}

    def at_y(t):
        return {"row": (x * ny + t) * CORES + c}

    def at_x(t):
        return {"row": (t * ny + y) * CORES + c}

    def push(stage, src, dst, target):
        s = STAGES.index(stage)
        pltpu.make_async_remote_copy(
            src_ref=src,
            dst_ref=dst,
            send_sem=send.at[s],
            recv_sem=recv.at[s],
            device_id=target,
            device_id_type=MESH,
        ).start()

    def landed(stage, ref):
        pltpu.make_async_copy(ref, ref, recv.at[STAGES.index(stage)]).wait()

    def sent(stage, ref):
        pltpu.make_async_copy(ref, ref, send.at[STAGES.index(stage)]).wait()

    def span(start, size, step=8):
        return pl.ds(pl.multiple_of(start, step), size)

    def rows_of(ref, start, size):
        return ref.at[span(start, size)]

    def each(n, fn):
        for t in sorted(range(1, n), key=lambda t: -min(t, n - t)):
            fn(t)

    barrier = pltpu.get_barrier_semaphore()

    def greet(target):
        pl.semaphore_signal(barrier, inc=1, device_id=target, device_id_type=MESH)

    def greet_z(t):
        greet(at_z(lax.rem(z + t, nz)))
        greet(at_z_other(lax.rem(z + t, nz)))

    each(nz, greet_z)
    load_m = pltpu.make_async_copy(m_hbm, m_ref, local.at[0])
    load_q = pltpu.make_async_copy(q_hbm, q_ref, local.at[1])
    load_m.start()
    load_q.start()
    each(ny, lambda t: greet(at_y(lax.rem(y + t, ny))))
    each(nx, lambda t: greet(at_x(lax.rem(x + t, nx))))
    greet(other)
    load_m.wait()
    load_q.wait()
    part[...] = dot(m_ref[...], q_ref[...])
    pl.semaphore_wait(barrier, 2 * nz + ny + nx - 3)

    def left_send(t):
        to = lax.rem(z + t, nz)
        push("left_rs", rows_of(part, to * piece, piece), rows_of(left_in, (t - 1) * piece, piece), at_z(to))

    each(nz, left_send)
    mine_cols = span(c * hcols, hcols, 128)
    other_cols = span((1 - c) * hcols, hcols, 128)
    push("m_core", m_ref.at[:, other_cols], m_other, other)
    landed("left_rs", left_in)
    total = part[span(z * piece, piece), :]
    for t in range(nz - 1):
        total = total + left_in[t * piece : (t + 1) * piece, :]
    left[span(z * piece, piece), :] = total
    mine = rows_of(left, z * piece, piece)
    each(nz, lambda t: push("left_ag", mine, mine, at_z(lax.rem(z + t, nz))))
    landed("left_ag", left_in)

    push("left_core", left, left_other, other)
    left_now = left[...]
    left_t = left_now.T
    gram_own = dot(left_t, left_now)
    w_half[...] = dot3(left_t, m_ref[:, mine_cols])
    landed("left_core", left_other)
    left_now = left_other[...]
    left_t = left_now.T
    gram_pair = gram_own + dot(left_t, left_now)
    gram_part[0:half, :] = gram_pair[0:half, 0:half]
    gram_part[half : 2 * half, :] = gram_pair[0:half, half:]
    gram_part[2 * half :, :] = gram_pair[half:, half:]

    def gram_y_send(t):
        to = lax.rem(y + t, ny)
        push(
            "gram_y",
            rows_of(gram_part, c * ghalf + to * gpiece, gpiece),
            rows_of(gram_y, (t - 1) * gpiece, gpiece),
            at_y(to),
        )

    each(ny, gram_y_send)
    landed("m_core", m_other)
    w_half[...] = w_half[...] + dot3(left_t, m_other[...])
    base_b = A_CHUNKS * p.chunk

    def a_piece(ref, base, k):
        return ref.at[
            span(base + lax.div(k, p.ay_split) * p.ay_rows, p.ay_rows),
            span(lax.rem(k, p.ay_split) * p.ay_cols, p.ay_cols, 128),
        ]

    def b_piece(ref, base, k):
        return ref.at[
            span(base + lax.div(k, p.bx_split) * p.bx_rows, p.bx_rows),
            span(lax.rem(k, p.bx_split) * p.bx_cols, p.bx_cols, 128),
        ]

    def a_start(i):
        def send_x(t):
            to = lax.rem(x + t, nx)
            push(
                f"wa{i}_x",
                rows_of(w_half, i * p.chunk + to * p.ax, p.ax),
                rows_of(wa_in.at[i], (t - 1) * p.ax, p.ax),
                at_x(to),
            )

        each(nx, send_x)

    def b_start():
        def send_y(t):
            to = lax.rem(y + t, ny)
            push("wb_y", rows_of(w_half, base_b + to * p.by, p.by), rows_of(wb_in, (t - 1) * p.by, p.by), at_y(to))

        each(ny, send_y)

    def a_second(i):
        def send_y(t):
            to = lax.rem(y + t, ny)
            push(
                f"wa{i}_y",
                a_piece(wa_sum.at[i], 0, to),
                rows_of(wa_piece_in.at[i], (t - 1) * p.ay_rows, p.ay_rows),
                at_y(to),
            )

        landed(f"wa{i}_x", wa_in.at[i])
        total = w_half[span(i * p.chunk + x * p.ax, p.ax), :]
        for t in range(nx - 1):
            total = total + wa_in[i, t * p.ax : (t + 1) * p.ax, :]
        wa_sum[i] = total
        each(ny, send_y)

    def b_second():
        def send_x(t):
            to = lax.rem(x + t, nx)
            push("wb_x", b_piece(wb_sum, 0, to), rows_of(wb_piece_in, (t - 1) * p.bx_rows, p.bx_rows), at_x(to))

        landed("wb_y", wb_in)
        total = w_half[span(base_b + y * p.by, p.by), :]
        for t in range(ny - 1):
            total = total + wb_in[t * p.by : (t + 1) * p.by, :]
        wb_sum[...] = total
        each(nx, send_x)

    def a_gather(i):
        landed(f"wa{i}_y", wa_piece_in.at[i])
        total = a_piece(wa_sum.at[i], 0, y)[...]
        for t in range(ny - 1):
            total = total + wa_piece_in[i, t * p.ay_rows : (t + 1) * p.ay_rows, :]
        mine_w = a_piece(w_full, i * p.chunk + x * p.ax, y)
        mine_w[...] = total
        each(ny, lambda t: push(f"wa{i}_yag", mine_w, mine_w, at_y(lax.rem(y + t, ny))))

    def b_gather():
        landed("wb_x", wb_piece_in)
        total = b_piece(wb_sum, 0, x)[...]
        for t in range(nx - 1):
            total = total + wb_piece_in[t * p.bx_rows : (t + 1) * p.bx_rows, :]
        mine_b = b_piece(w_full, base_b + y * p.by, x)
        mine_b[...] = total
        each(nx, lambda t: push("wb_xag", mine_b, mine_b, at_x(lax.rem(x + t, nx))))

    def a_last(i):
        landed(f"wa{i}_yag", wa_piece_in.at[i])
        rows_a = rows_of(w_full, i * p.chunk + x * p.ax, p.ax)
        each(nx, lambda t: push(f"wa{i}_xag", rows_a, rows_a, at_x(lax.rem(x + t, nx))))

    def b_last():
        landed("wb_xag", wb_piece_in)
        rows_b = rows_of(w_full, base_b + y * p.by, p.by)
        each(ny, lambda t: push("wb_yag", rows_b, rows_b, at_y(lax.rem(y + t, ny))))

    for i in range(A_CHUNKS):
        a_start(i)
    b_start()
    a_second(0)
    landed("gram_y", gram_y)
    total = gram_part[span(c * ghalf + y * gpiece, gpiece), :]
    for t in range(ny - 1):
        total = total + gram_y[t * gpiece : (t + 1) * gpiece, :]
    gram_x[span(x * gpiece, gpiece), :] = total
    mine_g = rows_of(gram_x, x * gpiece, gpiece)
    each(nx, lambda t: push("gram_x", mine_g, mine_g, at_x(lax.rem(x + t, nx))))
    for i in range(1, A_CHUNKS):
        a_second(i)
    b_second()
    landed("gram_x", gram_x.at[pl.ds(0, (nx - 1) * gpiece)])
    total = gram_x[0:gpiece, :]
    for t in range(1, nx):
        total = total + gram_x[t * gpiece : (t + 1) * gpiece, :]
    at = c * ghalf + y * gpiece
    gram[span(at, gpiece), :] = total
    mine_a = rows_of(gram, at, gpiece)
    each(ny, lambda t: push("gram_yag", mine_a, mine_a, at_y(lax.rem(y + t, ny))))
    a_gather(0)
    b_gather()
    for i in range(1, A_CHUNKS):
        a_gather(i)
    landed("gram_yag", gram_y)
    mine_h = rows_of(gram, c * ghalf, ghalf)
    push("gram_cag", mine_h, mine_h, other)
    b_last()
    a_last(0)
    landed("gram_cag", mine_h)

    nb = rank // BLOCK
    work[0:half, 0:half] = gram[0:half, :]
    work[0:half, half:] = gram[half : 2 * half, :]
    work[half:, 0:half] = jnp.zeros((half, half), jnp.float32)
    work[half:, half:] = gram[2 * half :, :]
    eye = (
        lax.broadcasted_iota(jnp.int32, (BLOCK, BLOCK), 0) == lax.broadcasted_iota(jnp.int32, (BLOCK, BLOCK), 1)
    ).astype(jnp.float32)

    def after_block(k):
        if k + 1 < A_CHUNKS:
            a_last(k + 1)

    inverse_rows = []
    solved = []
    for k in range(nb):
        lo, hi = k * BLOCK, (k + 1) * BLOCK
        diag = work[lo:hi, lo:hi]
        inv_kk = invert_cholesky_block(jnp.concatenate([diag, eye], axis=1))
        if hi < rank:
            u = dot(inv_kk, work[lo:hi, hi:])
            solved.append(u)
            work[hi:, hi:] = work[hi:, hi:] - dot(u, u, ((0,), (0,)))
        inv_row = inv_kk
        if k > 0:
            acc = None
            for i in range(k):
                term = dot(solved[i][:, lo - (i + 1) * BLOCK : lo - i * BLOCK], inverse_rows[i], ((0,), (0,)))
                width = (i + 1) * BLOCK
                if width < lo:
                    term = jnp.concatenate([term, jnp.zeros((BLOCK, lo - width), jnp.float32)], axis=1)
                acc = term if acc is None else acc + term
            inv_row = jnp.concatenate([-dot(inv_kk, acc), inv_kk], axis=1)
        inverse_rows.append(inv_row)
        if hi < rank:
            inv_row = jnp.concatenate([inv_row, jnp.zeros((BLOCK, rank - hi), jnp.float32)], axis=1)
        inverse_ref[lo:hi, :] = inv_row
        after_block(k)
    landed("wb_yag", wb_in)
    for i in range(A_CHUNKS):
        landed(f"wa{i}_xag", wa_in.at[i])
    r = dot3(inverse_ref[...], w_full[...])
    right[c] = r
    push("right_core", right.at[c], right.at[c], other)
    folded = r[:, 0:128] * r[:, 0:128]
    for t in range(1, hcols // 128):
        folded = folded + r[:, 128 * t : 128 * (t + 1)] * r[:, 128 * t : 128 * (t + 1)]
    squares = dot(jnp.ones((8, 128), jnp.float32), folded, ((1,), (1,)))
    norm_out[...] = squares[0:1, :]

    def norm_send(t):
        to = lax.rem(z + t, nz)
        push("norm", norm_out, norm_in.at[t - 1], at_z(to))
        push("norm", norm_out, norm_in.at[nz - 1 + t], at_z_other(to))

    each(nz, norm_send)
    push("norm", norm_out, norm_in.at[nz - 1], other)
    left_orth = dot(left[...], inverse_ref[...], ((1,), (1,)))
    half_orth = 0.5 * left_orth
    new_out[:, mine_cols] = m_ref[:, mine_cols] - dot3(half_orth, right[c])
    landed("right_core", w_half)
    new_out[:, other_cols] = m_ref[:, other_cols] - dot3(half_orth, right[1 - c])
    right_out[...] = right[...]
    landed("norm", norm_in)
    total = norm_out[...]
    for t in range(2 * nz - 1):
        total = total + norm_in[t]
    scale = math.sqrt(ROWS * COLS / RANK)
    left_out[...] = left_orth * (scale / jnp.sqrt(total + 1e-06))

    sent("left_rs", left_in)
    sent("left_ag", left_in)
    sent("m_core", m_other)
    sent("left_core", left_other)
    sent("gram_y", gram_y)
    sent("gram_x", gram_x.at[pl.ds(0, (nx - 1) * gpiece)])
    sent("gram_yag", gram_y)
    sent("gram_cag", mine_h)
    for i in range(A_CHUNKS):
        sent(f"wa{i}_x", wa_in.at[i])
        sent(f"wa{i}_y", wa_piece_in.at[i])
        sent(f"wa{i}_yag", wa_piece_in.at[i])
        sent(f"wa{i}_xag", wa_in.at[i])
    sent("wb_y", wb_in)
    sent("wb_x", wb_piece_in)
    sent("wb_xag", wb_piece_in)
    sent("wb_yag", wb_in)
    sent("right_core", w_half)
    sent("norm", norm_in)


def write_outputs(new_ref, right_ref, left_ref, new_hbm, upd_hbm, upd, sems):
    hcols = right_ref.shape[2]
    copies = [pltpu.make_async_copy(new_ref, new_hbm, sems.at[0])]
    copies[0].start()
    for h in range(2):
        at = pl.ds(h * hcols, hcols)
        upd[:, at] = dot3(left_ref[...], right_ref[h])
        copies.append(pltpu.make_async_copy(upd.at[:, at], upd_hbm.at[:, at], sems.at[1 + h]))
        copies[-1].start()
    for copy in copies:
        copy.wait()


def local_step(p, momentum, right_factor):
    f32 = jnp.float32
    vmem = lambda *shape: pltpu.VMEM(shape, f32)
    shaped = lambda *shape: jax.ShapeDtypeStruct(shape, f32)
    any_spec = pl.BlockSpec(memory_space=pl.ANY)
    hbm_spec = pl.BlockSpec(memory_space=pltpu.HBM)
    vmem_spec = pl.BlockSpec(memory_space=pltpu.VMEM)
    new, right, left = pl.pallas_call(
        functools.partial(kernel, p),
        out_shape=(shaped(p.rows, p.cols), shaped(2, p.rank, p.hcols), shaped(p.rows, p.rank)),
        in_specs=[hbm_spec, hbm_spec],
        out_specs=(vmem_spec,) * 3,
        scratch_shapes=[
            vmem(p.rows, p.cols),
            vmem(p.cols, p.rank),
            vmem(p.rows, p.rank),
            vmem(p.rows - p.piece, p.rank),
            vmem(p.rows, p.rank),
            vmem(p.rows, p.rank),
            vmem(p.rows, p.hcols),
            vmem(2 * p.ghalf, p.half),
            vmem(p.ghalf - p.gpiece, p.half),
            vmem(p.nx * p.gpiece, p.half),
            vmem(2 * p.ghalf, p.half),
            vmem(p.rank, p.rank),
            vmem(p.rank, p.hcols),
            vmem(A_CHUNKS, p.chunk - p.ax, p.hcols),
            vmem(A_CHUNKS, p.ax, p.hcols),
            vmem(A_CHUNKS, (p.ny - 1) * p.ay_rows, p.ay_cols),
            vmem(p.chunk - p.by, p.hcols),
            vmem(p.by, p.hcols),
            vmem((p.nx - 1) * p.bx_rows, p.bx_cols),
            vmem(p.rank, p.hcols),
            vmem(p.rank, p.rank),
            vmem(2, p.rank, p.hcols),
            vmem(2 * p.nz - 1, 1, p.rank),
            vmem(1, p.rank),
            pltpu.SemaphoreType.DMA((len(STAGES),)),
            pltpu.SemaphoreType.DMA((len(STAGES),)),
            pltpu.SemaphoreType.DMA((2,)),
        ],
        compiler_params=pltpu.CompilerParams(collective_id=0, has_side_effects=True, vmem_limit_bytes=VMEM_BYTES),
        name="dion",
    )(
        pltpu.with_memory_space_constraint(momentum, pltpu.HBM),
        pltpu.with_memory_space_constraint(right_factor, pltpu.HBM),
    )
    return pl.pallas_call(
        write_outputs,
        out_shape=(shaped(p.rows, p.cols),) * 2,
        in_specs=[vmem_spec] * 3,
        out_specs=(any_spec, any_spec),
        scratch_shapes=[vmem(p.rows, p.cols), pltpu.SemaphoreType.DMA((3,))],
        compiler_params=pltpu.CompilerParams(vmem_limit_bytes=8 * 2**20),
        name="outputs",
    )(new, right, left)


def solution(mesh):
    nz = mesh.shape["col"]
    ny = Y_CHIPS
    nx = mesh.shape["row"] // (ny * CORES)

    def local(momentum, right_factor):
        plan = Plan(nx, ny, nz, momentum.shape[0], momentum.shape[1], right_factor.shape[1])
        return local_step(plan, momentum, right_factor)

    in_specs = (P("row", "col"), P("col", None))
    out_specs = (P("row", "col"), P("row", "col"))
    return jax.shard_map(local, mesh=mesh, in_specs=in_specs, out_specs=out_specs, check_vma=False)
```

```python
import functools
import math

import jax
import jax.numpy as jnp
from jax import lax
from jax.experimental import pallas as pl
from jax.experimental.pallas import tpu as pltpu
from jax.sharding import PartitionSpec as P

ROWS = 8192
COLS = 16384
RANK = 256
CORES = 2
Y_CHIPS = 8
BLOCK = 64
WINDOW = 8
VMEM_BYTES = 24 * 2**20
HIGHEST = lax.Precision.HIGHEST
MESH = pl.DeviceIdType.MESH

A_CHUNKS = 3
STAGES = (
    ("left_rs", "left_ag", "m_core", "left_core", "gram_y", "gram_x", "gram_yag", "gram_cag")
    + tuple(f"wa{i}_{s}" for i in range(A_CHUNKS) for s in ("x", "y", "yag", "xag"))
    + ("wb_y", "wb_x", "wb_xag", "wb_yag", "right_core", "norm")
)


def dot(a, b, contract=((1,), (0,))):
    return lax.dot_general(
        a, b, (contract, ((), ())), precision=HIGHEST, preferred_element_type=jnp.float32
    )


def split(v):
    high = v.astype(jnp.bfloat16)
    return high, (v - high.astype(jnp.float32)).astype(jnp.bfloat16)


def dot3(a, b):
    a_high, a_low = split(a)
    b_high, b_low = split(b)

    def one(u, v):
        return lax.dot_general(u, v, (((1,), (0,)), ((), ())), preferred_element_type=jnp.float32)

    return one(a_high, b_high) + (one(a_high, b_low) + one(a_low, b_high))


def invert_cholesky_block(work):
    b = BLOCK
    groups = b // 8
    lanes = 2 * b
    rows8 = lax.broadcasted_iota(jnp.int32, (8, lanes), 0)
    a = [work[8 * g : 8 * g + 8, :] for g in range(groups)]
    pivots = [jnp.ones((8, lanes), jnp.float32) for _ in range(groups)]

    def spread(k):
        return {g: jnp.broadcast_to(a[g][:, k : k + 1], (8, lanes)) for g in range(k // 8, groups)}

    def sub(v, s):
        return jnp.broadcast_to(v[s : s + 1, :], (8, lanes))

    window = {k: spread(k) for k in range(WINDOW)}
    for j in range(b):
        gj, sj = divmod(j, 8)
        col = window.pop(j)
        pivot = sub(col[gj], sj)
        pivots[gj] = jnp.where(rows8 == sj, pivot, pivots[gj])
        if j == b - 1:
            break
        inv = 1.0 / pivot
        factor = {g: col[g] * inv for g in range((j + 1) // 8, groups)}
        for k in range(j + 1, min(j + WINDOW, b)):
            ahead = sub(col[k // 8], k % 8)
            for g in range(k // 8, groups):
                window[k][g] = window[k][g] - factor[g] * ahead
        row = sub(a[gj], sj)
        for g in range((j + 1) // 8, groups):
            f = factor[g]
            if g == gj:
                f = jnp.where(rows8 > sj, f, 0.0)
            a[g] = a[g] - f * row
        if j + WINDOW < b:
            window[j + WINDOW] = spread(j + WINDOW)
    out = [a[g] * lax.rsqrt(pivots[g]) for g in range(groups)]
    return jnp.concatenate(out, axis=0)[:, b:]


class Plan:
    def __init__(self, nx, ny, nz, rows, cols, rank):
        self.nx, self.ny, self.nz = nx, ny, nz
        self.rows, self.cols, self.rank = rows, cols, rank
        self.half = rank // 2
        self.hcols = cols // 2
        self.piece = rows // nz
        self.ghalf = 3 * self.half // 2
        self.gpiece = self.ghalf // ny
        self.chunk = rank // (A_CHUNKS + 1)
        self.ax = self.chunk // nx
        self.ay_rows = max(8, self.ax // ny)
        self.ay_split = ny * self.ay_rows // self.ax
        self.ay_cols = self.hcols // self.ay_split
        self.by = self.chunk // ny
        self.bx_rows = max(8, self.by // nx)
        self.bx_split = nx * self.bx_rows // self.by
        self.bx_cols = self.hcols // self.bx_split


def kernel(
    p,
    m_hbm,
    q_hbm,
    new_out,
    right_out,
    left_out,
    m_ref,
    q_ref,
    part,
    left_in,
    left,
    left_other,
    m_other,
    gram_part,
    gram_y,
    gram_x,
    gram,
    work,
    w_half,
    wa_in,
    wa_sum,
    wa_piece_in,
    wb_in,
    wb_sum,
    wb_piece_in,
    w_full,
    inverse_ref,
    right,
    norm_in,
    norm_out,
    send,
    recv,
    local,
):
    nx, ny, nz, rank = p.nx, p.ny, p.nz, p.rank
    half, hcols, piece, ghalf, gpiece = p.half, p.hcols, p.piece, p.ghalf, p.gpiece
    row_at = lax.axis_index("row")
    z = lax.axis_index("col")
    c = lax.rem(row_at, CORES)
    y = lax.rem(lax.div(row_at, CORES), ny)
    x = lax.div(row_at, CORES * ny)
    other_row = (x * ny + y) * CORES + (1 - c)
    other = {"row": other_row}

    def at_z(t):
        return {"col": t}

    def at_z_other(t):
        return {"row": other_row, "col": t}

    def at_y(t):
        return {"row": (x * ny + t) * CORES + c}

    def at_x(t):
        return {"row": (t * ny + y) * CORES + c}

    def push(stage, src, dst, target):
        s = STAGES.index(stage)
        pltpu.make_async_remote_copy(
            src_ref=src,
            dst_ref=dst,
            send_sem=send.at[s],
            recv_sem=recv.at[s],
            device_id=target,
            device_id_type=MESH,
        ).start()

    def landed(stage, ref):
        pltpu.make_async_copy(ref, ref, recv.at[STAGES.index(stage)]).wait()

    def sent(stage, ref):
        pltpu.make_async_copy(ref, ref, send.at[STAGES.index(stage)]).wait()

    def span(start, size, step=8):
        return pl.ds(pl.multiple_of(start, step), size)

    def rows_of(ref, start, size):
        return ref.at[span(start, size)]

    def each(n, fn):
        for t in sorted(range(1, n), key=lambda t: -min(t, n - t)):
            fn(t)

    barrier = pltpu.get_barrier_semaphore()

    def greet(target):
        pl.semaphore_signal(barrier, inc=1, device_id=target, device_id_type=MESH)

    def greet_z(t):
        greet(at_z(lax.rem(z + t, nz)))
        greet(at_z_other(lax.rem(z + t, nz)))

    each(nz, greet_z)
    load_m = pltpu.make_async_copy(m_hbm, m_ref, local.at[0])
    load_q = pltpu.make_async_copy(q_hbm, q_ref, local.at[1])
    load_m.start()
    load_q.start()
    each(ny, lambda t: greet(at_y(lax.rem(y + t, ny))))
    each(nx, lambda t: greet(at_x(lax.rem(x + t, nx))))
    greet(other)
    load_m.wait()
    load_q.wait()
    part[...] = dot(m_ref[...], q_ref[...])
    pl.semaphore_wait(barrier, 2 * nz + ny + nx - 3)

    def left_send(t):
        to = lax.rem(z + t, nz)
        push("left_rs", rows_of(part, to * piece, piece), rows_of(left_in, (t - 1) * piece, piece), at_z(to))

    each(nz, left_send)
    mine_cols = span(c * hcols, hcols, 128)
    other_cols = span((1 - c) * hcols, hcols, 128)
    push("m_core", m_ref.at[:, other_cols], m_other, other)
    landed("left_rs", left_in)
    total = part[span(z * piece, piece), :]
    for t in range(nz - 1):
        total = total + left_in[t * piece : (t + 1) * piece, :]
    left[span(z * piece, piece), :] = total
    mine = rows_of(left, z * piece, piece)
    each(nz, lambda t: push("left_ag", mine, mine, at_z(lax.rem(z + t, nz))))
    landed("left_ag", left_in)

    push("left_core", left, left_other, other)
    left_now = left[...]
    left_t = left_now.T
    w_half[...] = dot3(left_t, m_ref[:, mine_cols])
    gram_own = dot(left_t, left_now)
    landed("left_core", left_other)
    left_now = left_other[...]
    left_t = left_now.T
    landed("m_core", m_other)
    w_half[...] = w_half[...] + dot3(left_t, m_other[...])
    base_b = A_CHUNKS * p.chunk

    def a_piece(ref, base, k):
        return ref.at[
            span(base + lax.div(k, p.ay_split) * p.ay_rows, p.ay_rows),
            span(lax.rem(k, p.ay_split) * p.ay_cols, p.ay_cols, 128),
        ]

    def b_piece(ref, base, k):
        return ref.at[
            span(base + lax.div(k, p.bx_split) * p.bx_rows, p.bx_rows),
            span(lax.rem(k, p.bx_split) * p.bx_cols, p.bx_cols, 128),
        ]

    def a_start(i):
        def send_x(t):
            to = lax.rem(x + t, nx)
            push(
                f"wa{i}_x",
                rows_of(w_half, i * p.chunk + to * p.ax, p.ax),
                rows_of(wa_in.at[i], (t - 1) * p.ax, p.ax),
                at_x(to),
            )

        each(nx, send_x)

    def b_start():
        def send_y(t):
            to = lax.rem(y + t, ny)
            push("wb_y", rows_of(w_half, base_b + to * p.by, p.by), rows_of(wb_in, (t - 1) * p.by, p.by), at_y(to))

        each(ny, send_y)

    def a_second(i):
        def send_y(t):
            to = lax.rem(y + t, ny)
            push(
                f"wa{i}_y",
                a_piece(wa_sum.at[i], 0, to),
                rows_of(wa_piece_in.at[i], (t - 1) * p.ay_rows, p.ay_rows),
                at_y(to),
            )

        landed(f"wa{i}_x", wa_in.at[i])
        total = w_half[span(i * p.chunk + x * p.ax, p.ax), :]
        for t in range(nx - 1):
            total = total + wa_in[i, t * p.ax : (t + 1) * p.ax, :]
        wa_sum[i] = total
        each(ny, send_y)

    def b_second():
        def send_x(t):
            to = lax.rem(x + t, nx)
            push("wb_x", b_piece(wb_sum, 0, to), rows_of(wb_piece_in, (t - 1) * p.bx_rows, p.bx_rows), at_x(to))

        landed("wb_y", wb_in)
        total = w_half[span(base_b + y * p.by, p.by), :]
        for t in range(ny - 1):
            total = total + wb_in[t * p.by : (t + 1) * p.by, :]
        wb_sum[...] = total
        each(nx, send_x)

    def a_gather(i):
        landed(f"wa{i}_y", wa_piece_in.at[i])
        total = a_piece(wa_sum.at[i], 0, y)[...]
        for t in range(ny - 1):
            total = total + wa_piece_in[i, t * p.ay_rows : (t + 1) * p.ay_rows, :]
        mine_w = a_piece(w_full, i * p.chunk + x * p.ax, y)
        mine_w[...] = total
        each(ny, lambda t: push(f"wa{i}_yag", mine_w, mine_w, at_y(lax.rem(y + t, ny))))

    def b_gather():
        landed("wb_x", wb_piece_in)
        total = b_piece(wb_sum, 0, x)[...]
        for t in range(nx - 1):
            total = total + wb_piece_in[t * p.bx_rows : (t + 1) * p.bx_rows, :]
        mine_b = b_piece(w_full, base_b + y * p.by, x)
        mine_b[...] = total
        each(nx, lambda t: push("wb_xag", mine_b, mine_b, at_x(lax.rem(x + t, nx))))

    def a_last(i):
        landed(f"wa{i}_yag", wa_piece_in.at[i])
        rows_a = rows_of(w_full, i * p.chunk + x * p.ax, p.ax)
        each(nx, lambda t: push(f"wa{i}_xag", rows_a, rows_a, at_x(lax.rem(x + t, nx))))

    def b_last():
        landed("wb_xag", wb_piece_in)
        rows_b = rows_of(w_full, base_b + y * p.by, p.by)
        each(ny, lambda t: push("wb_yag", rows_b, rows_b, at_y(lax.rem(y + t, ny))))

    for i in range(A_CHUNKS):
        a_start(i)
    gram_pair = gram_own + dot(left_t, left_now)
    gram_part[0:half, :] = gram_pair[0:half, 0:half]
    gram_part[half : 2 * half, :] = gram_pair[0:half, half:]
    gram_part[2 * half :, :] = gram_pair[half:, half:]

    def gram_y_send(t):
        to = lax.rem(y + t, ny)
        push(
            "gram_y",
            rows_of(gram_part, c * ghalf + to * gpiece, gpiece),
            rows_of(gram_y, (t - 1) * gpiece, gpiece),
            at_y(to),
        )

    each(ny, gram_y_send)
    b_start()
    a_second(0)
    landed("gram_y", gram_y)
    total = gram_part[span(c * ghalf + y * gpiece, gpiece), :]
    for t in range(ny - 1):
        total = total + gram_y[t * gpiece : (t + 1) * gpiece, :]
    gram_x[span(x * gpiece, gpiece), :] = total
    mine_g = rows_of(gram_x, x * gpiece, gpiece)
    each(nx, lambda t: push("gram_x", mine_g, mine_g, at_x(lax.rem(x + t, nx))))
    for i in range(1, A_CHUNKS):
        a_second(i)
    b_second()
    landed("gram_x", gram_x.at[pl.ds(0, (nx - 1) * gpiece)])
    total = gram_x[0:gpiece, :]
    for t in range(1, nx):
        total = total + gram_x[t * gpiece : (t + 1) * gpiece, :]
    at = c * ghalf + y * gpiece
    gram[span(at, gpiece), :] = total
    mine_a = rows_of(gram, at, gpiece)
    each(ny, lambda t: push("gram_yag", mine_a, mine_a, at_y(lax.rem(y + t, ny))))
    a_gather(0)
    b_gather()
    for i in range(1, A_CHUNKS):
        a_gather(i)
    landed("gram_yag", gram_y)
    mine_h = rows_of(gram, c * ghalf, ghalf)
    push("gram_cag", mine_h, mine_h, other)
    b_last()
    a_last(0)
    landed("gram_cag", mine_h)

    nb = rank // BLOCK
    work[0:half, 0:half] = gram[0:half, :]
    work[0:half, half:] = gram[half : 2 * half, :]
    work[half:, 0:half] = jnp.zeros((half, half), jnp.float32)
    work[half:, half:] = gram[2 * half :, :]
    eye = (
        lax.broadcasted_iota(jnp.int32, (BLOCK, BLOCK), 0) == lax.broadcasted_iota(jnp.int32, (BLOCK, BLOCK), 1)
    ).astype(jnp.float32)

    def after_block(k):
        if k + 1 < A_CHUNKS:
            a_last(k + 1)

    inverse_rows = []
    solved = []
    for k in range(nb):
        lo, hi = k * BLOCK, (k + 1) * BLOCK
        diag = work[lo:hi, lo:hi]
        inv_kk = invert_cholesky_block(jnp.concatenate([diag, eye], axis=1))
        if hi < rank:
            u = dot(inv_kk, work[lo:hi, hi:])
            solved.append(u)
            work[hi:, hi:] = work[hi:, hi:] - dot(u, u, ((0,), (0,)))
        inv_row = inv_kk
        if k > 0:
            acc = None
            for i in range(k):
                term = dot(solved[i][:, lo - (i + 1) * BLOCK : lo - i * BLOCK], inverse_rows[i], ((0,), (0,)))
                width = (i + 1) * BLOCK
                if width < lo:
                    term = jnp.concatenate([term, jnp.zeros((BLOCK, lo - width), jnp.float32)], axis=1)
                acc = term if acc is None else acc + term
            inv_row = jnp.concatenate([-dot(inv_kk, acc), inv_kk], axis=1)
        inverse_rows.append(inv_row)
        if hi < rank:
            inv_row = jnp.concatenate([inv_row, jnp.zeros((BLOCK, rank - hi), jnp.float32)], axis=1)
        inverse_ref[lo:hi, :] = inv_row
        after_block(k)
    for i in range(2):
        landed(f"wa{i}_xag", wa_in.at[i])
    first = 2 * p.chunk
    r = dot3(inverse_ref[:, 0:first], w_full[0:first, :])
    landed("wb_yag", wb_in)
    for i in range(2, A_CHUNKS):
        landed(f"wa{i}_xag", wa_in.at[i])
    r = r + dot3(inverse_ref[:, first:], w_full[first:, :])
    right[c] = r
    push("right_core", right.at[c], right.at[c], other)
    folded = r[:, 0:128] * r[:, 0:128]
    for t in range(1, hcols // 128):
        folded = folded + r[:, 128 * t : 128 * (t + 1)] * r[:, 128 * t : 128 * (t + 1)]
    squares = dot(jnp.ones((8, 128), jnp.float32), folded, ((1,), (1,)))
    norm_out[...] = squares[0:1, :]

    def norm_send(t):
        to = lax.rem(z + t, nz)
        push("norm", norm_out, norm_in.at[t - 1], at_z(to))
        push("norm", norm_out, norm_in.at[nz - 1 + t], at_z_other(to))

    each(nz, norm_send)
    push("norm", norm_out, norm_in.at[nz - 1], other)
    left_orth = dot(left[...], inverse_ref[...], ((1,), (1,)))
    half_orth = 0.5 * left_orth
    new_out[:, mine_cols] = m_ref[:, mine_cols] - dot3(half_orth, right[c])
    landed("right_core", w_half)
    new_out[:, other_cols] = m_ref[:, other_cols] - dot3(half_orth, right[1 - c])
    right_out[...] = right[...]
    landed("norm", norm_in)
    total = norm_out[...]
    for t in range(2 * nz - 1):
        total = total + norm_in[t]
    scale = math.sqrt(ROWS * COLS / RANK)
    left_out[...] = left_orth * (scale / jnp.sqrt(total + 1e-06))

    sent("left_rs", left_in)
    sent("left_ag", left_in)
    sent("m_core", m_other)
    sent("left_core", left_other)
    sent("gram_y", gram_y)
    sent("gram_x", gram_x.at[pl.ds(0, (nx - 1) * gpiece)])
    sent("gram_yag", gram_y)
    sent("gram_cag", mine_h)
    for i in range(A_CHUNKS):
        sent(f"wa{i}_x", wa_in.at[i])
        sent(f"wa{i}_y", wa_piece_in.at[i])
        sent(f"wa{i}_yag", wa_piece_in.at[i])
        sent(f"wa{i}_xag", wa_in.at[i])
    sent("wb_y", wb_in)
    sent("wb_x", wb_piece_in)
    sent("wb_xag", wb_piece_in)
    sent("wb_yag", wb_in)
    sent("right_core", w_half)
    sent("norm", norm_in)


def write_outputs(new_ref, right_ref, left_ref, new_hbm, upd_hbm, upd, sems):
    hcols = right_ref.shape[2]
    copies = [pltpu.make_async_copy(new_ref, new_hbm, sems.at[0])]
    copies[0].start()
    for h in range(2):
        at = pl.ds(h * hcols, hcols)
        upd[:, at] = dot3(left_ref[...], right_ref[h])
        copies.append(pltpu.make_async_copy(upd.at[:, at], upd_hbm.at[:, at], sems.at[1 + h]))
        copies[-1].start()
    for copy in copies:
        copy.wait()


def local_step(p, momentum, right_factor):
    f32 = jnp.float32
    vmem = lambda *shape: pltpu.VMEM(shape, f32)
    shaped = lambda *shape: jax.ShapeDtypeStruct(shape, f32)
    any_spec = pl.BlockSpec(memory_space=pl.ANY)
    hbm_spec = pl.BlockSpec(memory_space=pltpu.HBM)
    vmem_spec = pl.BlockSpec(memory_space=pltpu.VMEM)
    new, right, left = pl.pallas_call(
        functools.partial(kernel, p),
        out_shape=(shaped(p.rows, p.cols), shaped(2, p.rank, p.hcols), shaped(p.rows, p.rank)),
        in_specs=[hbm_spec, hbm_spec],
        out_specs=(vmem_spec,) * 3,
        scratch_shapes=[
            vmem(p.rows, p.cols),
            vmem(p.cols, p.rank),
            vmem(p.rows, p.rank),
            vmem(p.rows - p.piece, p.rank),
            vmem(p.rows, p.rank),
            vmem(p.rows, p.rank),
            vmem(p.rows, p.hcols),
            vmem(2 * p.ghalf, p.half),
            vmem(p.ghalf - p.gpiece, p.half),
            vmem(p.nx * p.gpiece, p.half),
            vmem(2 * p.ghalf, p.half),
            vmem(p.rank, p.rank),
            vmem(p.rank, p.hcols),
            vmem(A_CHUNKS, p.chunk - p.ax, p.hcols),
            vmem(A_CHUNKS, p.ax, p.hcols),
            vmem(A_CHUNKS, (p.ny - 1) * p.ay_rows, p.ay_cols),
            vmem(p.chunk - p.by, p.hcols),
            vmem(p.by, p.hcols),
            vmem((p.nx - 1) * p.bx_rows, p.bx_cols),
            vmem(p.rank, p.hcols),
            vmem(p.rank, p.rank),
            vmem(2, p.rank, p.hcols),
            vmem(2 * p.nz - 1, 1, p.rank),
            vmem(1, p.rank),
            pltpu.SemaphoreType.DMA((len(STAGES),)),
            pltpu.SemaphoreType.DMA((len(STAGES),)),
            pltpu.SemaphoreType.DMA((2,)),
        ],
        compiler_params=pltpu.CompilerParams(collective_id=0, has_side_effects=True, vmem_limit_bytes=VMEM_BYTES),
        name="dion",
    )(
        pltpu.with_memory_space_constraint(momentum, pltpu.HBM),
        pltpu.with_memory_space_constraint(right_factor, pltpu.HBM),
    )
    return pl.pallas_call(
        write_outputs,
        out_shape=(shaped(p.rows, p.cols),) * 2,
        in_specs=[vmem_spec] * 3,
        out_specs=(any_spec, any_spec),
        scratch_shapes=[vmem(p.rows, p.cols), pltpu.SemaphoreType.DMA((3,))],
        compiler_params=pltpu.CompilerParams(vmem_limit_bytes=8 * 2**20),
        name="outputs",
    )(new, right, left)


def solution(mesh):
    nz = mesh.shape["col"]
    ny = Y_CHIPS
    nx = mesh.shape["row"] // (ny * CORES)

    def local(momentum, right_factor):
        plan = Plan(nx, ny, nz, momentum.shape[0], momentum.shape[1], right_factor.shape[1])
        return local_step(plan, momentum, right_factor)

    in_specs = (P("row", "col"), P("col", None))
    out_specs = (P("row", "col"), P("row", "col"))
    return jax.shard_map(local, mesh=mesh, in_specs=in_specs, out_specs=out_specs, check_vma=False)
```

```python
import functools
import math

import jax
import jax.numpy as jnp
from jax import lax
from jax.experimental import pallas as pl
from jax.experimental.pallas import tpu as pltpu
from jax.sharding import PartitionSpec as P

ROWS = 8192
COLS = 16384
RANK = 256
CORES = 2
Y_CHIPS = 8
BLOCK = 64
WINDOW = 8
VMEM_BYTES = 24 * 2**20
HIGHEST = lax.Precision.HIGHEST
MESH = pl.DeviceIdType.MESH

A_CHUNKS = 3
STAGES = (
    ("left_rs", "left_ag", "m_core", "left_core", "gram_y", "gram_x", "gram_yag", "gram_cag")
    + tuple(f"wa{i}_{s}" for i in range(A_CHUNKS) for s in ("x", "y", "yag", "xag"))
    + ("wb_y", "wb_x", "wb_xag", "wb_yag", "right_core", "norm")
)


def dot(a, b, contract=((1,), (0,))):
    return lax.dot_general(
        a, b, (contract, ((), ())), precision=HIGHEST, preferred_element_type=jnp.float32
    )


def split(v):
    high = v.astype(jnp.bfloat16)
    return high, (v - high.astype(jnp.float32)).astype(jnp.bfloat16)


def dot3(a, b):
    a_high, a_low = split(a)
    b_high, b_low = split(b)

    def one(u, v):
        return lax.dot_general(u, v, (((1,), (0,)), ((), ())), preferred_element_type=jnp.float32)

    return one(a_high, b_high) + (one(a_high, b_low) + one(a_low, b_high))


def invert_cholesky_block(work):
    b = BLOCK
    groups = b // 8
    lanes = 2 * b
    rows8 = lax.broadcasted_iota(jnp.int32, (8, lanes), 0)
    a = [work[8 * g : 8 * g + 8, :] for g in range(groups)]
    pivots = [jnp.ones((8, lanes), jnp.float32) for _ in range(groups)]

    def spread(k):
        return {g: jnp.broadcast_to(a[g][:, k : k + 1], (8, lanes)) for g in range(k // 8, groups)}

    def sub(v, s):
        return jnp.broadcast_to(v[s : s + 1, :], (8, lanes))

    window = {k: spread(k) for k in range(WINDOW)}
    for j in range(b):
        gj, sj = divmod(j, 8)
        col = window.pop(j)
        pivot = sub(col[gj], sj)
        pivots[gj] = jnp.where(rows8 == sj, pivot, pivots[gj])
        if j == b - 1:
            break
        inv = 1.0 / pivot
        factor = {g: col[g] * inv for g in range((j + 1) // 8, groups)}
        for k in range(j + 1, min(j + WINDOW, b)):
            ahead = sub(col[k // 8], k % 8)
            for g in range(k // 8, groups):
                window[k][g] = window[k][g] - factor[g] * ahead
        row = sub(a[gj], sj)
        for g in range((j + 1) // 8, groups):
            f = factor[g]
            if g == gj:
                f = jnp.where(rows8 > sj, f, 0.0)
            a[g] = a[g] - f * row
        if j + WINDOW < b:
            window[j + WINDOW] = spread(j + WINDOW)
    out = [a[g] * lax.rsqrt(pivots[g]) for g in range(groups)]
    return jnp.concatenate(out, axis=0)[:, b:]


class Plan:
    def __init__(self, nx, ny, nz, rows, cols, rank):
        self.nx, self.ny, self.nz = nx, ny, nz
        self.rows, self.cols, self.rank = rows, cols, rank
        self.half = rank // 2
        self.hcols = cols // 2
        self.piece = rows // nz
        self.ghalf = 3 * self.half // 2
        self.gpiece = self.ghalf // ny
        self.chunk = rank // (A_CHUNKS + 1)
        self.ax = self.chunk // nx
        self.ay_rows = max(8, self.ax // ny)
        self.ay_split = ny * self.ay_rows // self.ax
        self.ay_cols = self.hcols // self.ay_split
        self.by = self.chunk // ny
        self.bx_rows = max(8, self.by // nx)
        self.bx_split = nx * self.bx_rows // self.by
        self.bx_cols = self.hcols // self.bx_split


def kernel(
    p,
    m_hbm,
    q_hbm,
    new_out,
    right_out,
    left_out,
    m_ref,
    q_ref,
    part,
    left_in,
    left,
    left_other,
    m_other,
    gram_part,
    gram_y,
    gram_x,
    gram,
    work,
    w_half,
    wa_in,
    wa_sum,
    wa_piece_in,
    wb_in,
    wb_sum,
    wb_piece_in,
    w_full,
    inverse_ref,
    right,
    norm_in,
    norm_out,
    send,
    recv,
    local,
):
    nx, ny, nz, rank = p.nx, p.ny, p.nz, p.rank
    half, hcols, piece, ghalf, gpiece = p.half, p.hcols, p.piece, p.ghalf, p.gpiece
    row_at = lax.axis_index("row")
    z = lax.axis_index("col")
    c = lax.rem(row_at, CORES)
    y = lax.rem(lax.div(row_at, CORES), ny)
    x = lax.div(row_at, CORES * ny)
    other_row = (x * ny + y) * CORES + (1 - c)
    other = {"row": other_row}

    def at_z(t):
        return {"col": t}

    def at_z_other(t):
        return {"row": other_row, "col": t}

    def at_y(t):
        return {"row": (x * ny + t) * CORES + c}

    def at_x(t):
        return {"row": (t * ny + y) * CORES + c}

    def push(stage, src, dst, target):
        s = STAGES.index(stage)
        pltpu.make_async_remote_copy(
            src_ref=src,
            dst_ref=dst,
            send_sem=send.at[s],
            recv_sem=recv.at[s],
            device_id=target,
            device_id_type=MESH,
        ).start()

    def landed(stage, ref):
        pltpu.make_async_copy(ref, ref, recv.at[STAGES.index(stage)]).wait()

    def sent(stage, ref):
        pltpu.make_async_copy(ref, ref, send.at[STAGES.index(stage)]).wait()

    def span(start, size, step=8):
        return pl.ds(pl.multiple_of(start, step), size)

    def rows_of(ref, start, size):
        return ref.at[span(start, size)]

    def each(n, fn):
        for t in sorted(range(1, n), key=lambda t: -min(t, n - t)):
            fn(t)

    barrier = pltpu.get_barrier_semaphore()

    def greet(target):
        pl.semaphore_signal(barrier, inc=1, device_id=target, device_id_type=MESH)

    def greet_z(t):
        greet(at_z(lax.rem(z + t, nz)))
        greet(at_z_other(lax.rem(z + t, nz)))

    each(nz, greet_z)
    load_m = pltpu.make_async_copy(m_hbm, m_ref, local.at[0])
    load_q = pltpu.make_async_copy(q_hbm, q_ref, local.at[1])
    load_m.start()
    load_q.start()
    each(ny, lambda t: greet(at_y(lax.rem(y + t, ny))))
    each(nx, lambda t: greet(at_x(lax.rem(x + t, nx))))
    greet(other)
    load_m.wait()
    load_q.wait()
    part[...] = dot(m_ref[...], q_ref[...])
    pl.semaphore_wait(barrier, 2 * nz + ny + nx - 3)

    def left_send(t):
        to = lax.rem(z + t, nz)
        push("left_rs", rows_of(part, to * piece, piece), rows_of(left_in, (t - 1) * piece, piece), at_z(to))

    each(nz, left_send)
    mine_cols = span(c * hcols, hcols, 128)
    other_cols = span((1 - c) * hcols, hcols, 128)
    push("m_core", m_ref.at[:, other_cols], m_other, other)
    landed("left_rs", left_in)
    total = part[span(z * piece, piece), :]
    for t in range(nz - 1):
        total = total + left_in[t * piece : (t + 1) * piece, :]
    left[span(z * piece, piece), :] = total
    mine = rows_of(left, z * piece, piece)
    each(nz, lambda t: push("left_ag", mine, mine, at_z(lax.rem(z + t, nz))))
    landed("left_ag", left_in)

    push("left_core", left, left_other, other)
    left_now = left[...]
    left_t = left_now.T
    gram_own = dot(left_t, left_now)
    w_half[...] = dot3(left_t, m_ref[:, mine_cols])
    landed("left_core", left_other)
    left_now = left_other[...]
    left_t = left_now.T
    gram_pair = gram_own + dot(left_t, left_now)
    gram_part[0:half, :] = gram_pair[0:half, 0:half]
    gram_part[half : 2 * half, :] = gram_pair[0:half, half:]
    gram_part[2 * half :, :] = gram_pair[half:, half:]

    def gram_y_send(t):
        to = lax.rem(y + t, ny)
        push(
            "gram_y",
            rows_of(gram_part, c * ghalf + to * gpiece, gpiece),
            rows_of(gram_y, (t - 1) * gpiece, gpiece),
            at_y(to),
        )

    each(ny, gram_y_send)
    landed("m_core", m_other)
    w_half[...] = w_half[...] + dot3(left_t, m_other[...])
    base_b = A_CHUNKS * p.chunk

    def a_piece(ref, base, k):
        return ref.at[
            span(base + lax.div(k, p.ay_split) * p.ay_rows, p.ay_rows),
            span(lax.rem(k, p.ay_split) * p.ay_cols, p.ay_cols, 128),
        ]

    def b_piece(ref, base, k):
        return ref.at[
            span(base + lax.div(k, p.bx_split) * p.bx_rows, p.bx_rows),
            span(lax.rem(k, p.bx_split) * p.bx_cols, p.bx_cols, 128),
        ]

    def a_start(i):
        def send_x(t):
            to = lax.rem(x + t, nx)
            push(
                f"wa{i}_x",
                rows_of(w_half, i * p.chunk + to * p.ax, p.ax),
                rows_of(wa_in.at[i], (t - 1) * p.ax, p.ax),
                at_x(to),
            )

        each(nx, send_x)

    def b_start():
        def send_y(t):
            to = lax.rem(y + t, ny)
            push("wb_y", rows_of(w_half, base_b + to * p.by, p.by), rows_of(wb_in, (t - 1) * p.by, p.by), at_y(to))

        each(ny, send_y)

    def a_second(i):
        def send_y(t):
            to = lax.rem(y + t, ny)
            push(
                f"wa{i}_y",
                a_piece(wa_sum.at[i], 0, to),
                rows_of(wa_piece_in.at[i], (t - 1) * p.ay_rows, p.ay_rows),
                at_y(to),
            )

        landed(f"wa{i}_x", wa_in.at[i])
        total = w_half[span(i * p.chunk + x * p.ax, p.ax), :]
        for t in range(nx - 1):
            total = total + wa_in[i, t * p.ax : (t + 1) * p.ax, :]
        wa_sum[i] = total
        each(ny, send_y)

    def b_second():
        def send_x(t):
            to = lax.rem(x + t, nx)
            push("wb_x", b_piece(wb_sum, 0, to), rows_of(wb_piece_in, (t - 1) * p.bx_rows, p.bx_rows), at_x(to))

        landed("wb_y", wb_in)
        total = w_half[span(base_b + y * p.by, p.by), :]
        for t in range(ny - 1):
            total = total + wb_in[t * p.by : (t + 1) * p.by, :]
        wb_sum[...] = total
        each(nx, send_x)

    def a_gather(i):
        landed(f"wa{i}_y", wa_piece_in.at[i])
        total = a_piece(wa_sum.at[i], 0, y)[...]
        for t in range(ny - 1):
            total = total + wa_piece_in[i, t * p.ay_rows : (t + 1) * p.ay_rows, :]
        mine_w = a_piece(w_full, i * p.chunk + x * p.ax, y)
        mine_w[...] = total
        each(ny, lambda t: push(f"wa{i}_yag", mine_w, mine_w, at_y(lax.rem(y + t, ny))))

    def b_gather():
        landed("wb_x", wb_piece_in)
        total = b_piece(wb_sum, 0, x)[...]
        for t in range(nx - 1):
            total = total + wb_piece_in[t * p.bx_rows : (t + 1) * p.bx_rows, :]
        mine_b = b_piece(w_full, base_b + y * p.by, x)
        mine_b[...] = total
        each(nx, lambda t: push("wb_xag", mine_b, mine_b, at_x(lax.rem(x + t, nx))))

    def a_last(i):
        landed(f"wa{i}_yag", wa_piece_in.at[i])
        rows_a = rows_of(w_full, i * p.chunk + x * p.ax, p.ax)
        each(nx, lambda t: push(f"wa{i}_xag", rows_a, rows_a, at_x(lax.rem(x + t, nx))))

    def b_last():
        landed("wb_xag", wb_piece_in)
        rows_b = rows_of(w_full, base_b + y * p.by, p.by)
        each(ny, lambda t: push("wb_yag", rows_b, rows_b, at_y(lax.rem(y + t, ny))))

    for i in range(A_CHUNKS):
        a_start(i)
    b_start()
    a_second(0)
    landed("gram_y", gram_y)
    total = gram_part[span(c * ghalf + y * gpiece, gpiece), :]
    for t in range(ny - 1):
        total = total + gram_y[t * gpiece : (t + 1) * gpiece, :]
    gram_x[span(x * gpiece, gpiece), :] = total
    mine_g = rows_of(gram_x, x * gpiece, gpiece)
    each(nx, lambda t: push("gram_x", mine_g, mine_g, at_x(lax.rem(x + t, nx))))
    for i in range(1, A_CHUNKS):
        a_second(i)
    b_second()
    landed("gram_x", gram_x.at[pl.ds(0, (nx - 1) * gpiece)])
    total = gram_x[0:gpiece, :]
    for t in range(1, nx):
        total = total + gram_x[t * gpiece : (t + 1) * gpiece, :]
    at = c * ghalf + y * gpiece
    gram[span(at, gpiece), :] = total
    mine_a = rows_of(gram, at, gpiece)
    each(ny, lambda t: push("gram_yag", mine_a, mine_a, at_y(lax.rem(y + t, ny))))
    a_gather(0)
    b_gather()
    for i in range(1, A_CHUNKS):
        a_gather(i)
    landed("gram_yag", gram_y)
    mine_h = rows_of(gram, c * ghalf, ghalf)
    push("gram_cag", mine_h, mine_h, other)
    b_last()
    a_last(0)
    landed("gram_cag", mine_h)

    nb = rank // BLOCK
    work[0:half, 0:half] = gram[0:half, :]
    work[0:half, half:] = gram[half : 2 * half, :]
    work[half:, 0:half] = jnp.zeros((half, half), jnp.float32)
    work[half:, half:] = gram[2 * half :, :]
    eye = (
        lax.broadcasted_iota(jnp.int32, (BLOCK, BLOCK), 0) == lax.broadcasted_iota(jnp.int32, (BLOCK, BLOCK), 1)
    ).astype(jnp.float32)

    def after_block(k):
        if k + 1 < A_CHUNKS:
            a_last(k + 1)

    inverse_rows = []
    solved = []
    for k in range(nb):
        lo, hi = k * BLOCK, (k + 1) * BLOCK
        diag = work[lo:hi, lo:hi]
        inv_kk = invert_cholesky_block(jnp.concatenate([diag, eye], axis=1))
        if hi < rank:
            u = dot(inv_kk, work[lo:hi, hi:])
            solved.append(u)
            work[hi:, hi:] = work[hi:, hi:] - dot(u, u, ((0,), (0,)))
        inv_row = inv_kk
        if k > 0:
            acc = None
            for i in range(k):
                term = dot(solved[i][:, lo - (i + 1) * BLOCK : lo - i * BLOCK], inverse_rows[i], ((0,), (0,)))
                width = (i + 1) * BLOCK
                if width < lo:
                    term = jnp.concatenate([term, jnp.zeros((BLOCK, lo - width), jnp.float32)], axis=1)
                acc = term if acc is None else acc + term
            inv_row = jnp.concatenate([-dot(inv_kk, acc), inv_kk], axis=1)
        inverse_rows.append(inv_row)
        if hi < rank:
            inv_row = jnp.concatenate([inv_row, jnp.zeros((BLOCK, rank - hi), jnp.float32)], axis=1)
        inverse_ref[lo:hi, :] = inv_row
        after_block(k)
    for i in range(2):
        landed(f"wa{i}_xag", wa_in.at[i])
    first = 2 * p.chunk
    r = dot3(inverse_ref[:, 0:first], w_full[0:first, :])
    landed("wb_yag", wb_in)
    for i in range(2, A_CHUNKS):
        landed(f"wa{i}_xag", wa_in.at[i])
    r = r + dot3(inverse_ref[:, first:], w_full[first:, :])
    right[c] = r
    push("right_core", right.at[c], right.at[c], other)
    folded = r[:, 0:128] * r[:, 0:128]
    for t in range(1, hcols // 128):
        folded = folded + r[:, 128 * t : 128 * (t + 1)] * r[:, 128 * t : 128 * (t + 1)]
    squares = dot(jnp.ones((8, 128), jnp.float32), folded, ((1,), (1,)))
    norm_out[...] = squares[0:1, :]

    def norm_send(t):
        to = lax.rem(z + t, nz)
        push("norm", norm_out, norm_in.at[t - 1], at_z(to))
        push("norm", norm_out, norm_in.at[nz - 1 + t], at_z_other(to))

    each(nz, norm_send)
    push("norm", norm_out, norm_in.at[nz - 1], other)
    left_orth = dot(left[...], inverse_ref[...], ((1,), (1,)))
    half_orth = 0.5 * left_orth
    new_out[:, mine_cols] = m_ref[:, mine_cols] - dot3(half_orth, right[c])
    landed("right_core", w_half)
    new_out[:, other_cols] = m_ref[:, other_cols] - dot3(half_orth, right[1 - c])
    right_out[...] = right[...]
    landed("norm", norm_in)
    total = norm_out[...]
    for t in range(2 * nz - 1):
        total = total + norm_in[t]
    scale = math.sqrt(ROWS * COLS / RANK)
    left_out[...] = left_orth * (scale / jnp.sqrt(total + 1e-06))

    sent("left_rs", left_in)
    sent("left_ag", left_in)
    sent("m_core", m_other)
    sent("left_core", left_other)
    sent("gram_y", gram_y)
    sent("gram_x", gram_x.at[pl.ds(0, (nx - 1) * gpiece)])
    sent("gram_yag", gram_y)
    sent("gram_cag", mine_h)
    for i in range(A_CHUNKS):
        sent(f"wa{i}_x", wa_in.at[i])
        sent(f"wa{i}_y", wa_piece_in.at[i])
        sent(f"wa{i}_yag", wa_piece_in.at[i])
        sent(f"wa{i}_xag", wa_in.at[i])
    sent("wb_y", wb_in)
    sent("wb_x", wb_piece_in)
    sent("wb_xag", wb_piece_in)
    sent("wb_yag", wb_in)
    sent("right_core", w_half)
    sent("norm", norm_in)


def write_outputs(new_ref, right_ref, left_ref, new_hbm, upd_hbm, upd, sems):
    hcols = right_ref.shape[2]
    copies = [pltpu.make_async_copy(new_ref, new_hbm, sems.at[0])]
    copies[0].start()
    for h in range(2):
        at = pl.ds(h * hcols, hcols)
        upd[:, at] = dot3(left_ref[...], right_ref[h])
        copies.append(pltpu.make_async_copy(upd.at[:, at], upd_hbm.at[:, at], sems.at[1 + h]))
        copies[-1].start()
    for copy in copies:
        copy.wait()


def local_step(p, momentum, right_factor):
    f32 = jnp.float32
    vmem = lambda *shape: pltpu.VMEM(shape, f32)
    shaped = lambda *shape: jax.ShapeDtypeStruct(shape, f32)
    any_spec = pl.BlockSpec(memory_space=pl.ANY)
    hbm_spec = pl.BlockSpec(memory_space=pltpu.HBM)
    vmem_spec = pl.BlockSpec(memory_space=pltpu.VMEM)
    new, right, left = pl.pallas_call(
        functools.partial(kernel, p),
        out_shape=(shaped(p.rows, p.cols), shaped(2, p.rank, p.hcols), shaped(p.rows, p.rank)),
        in_specs=[hbm_spec, hbm_spec],
        out_specs=(vmem_spec,) * 3,
        scratch_shapes=[
            vmem(p.rows, p.cols),
            vmem(p.cols, p.rank),
            vmem(p.rows, p.rank),
            vmem(p.rows - p.piece, p.rank),
            vmem(p.rows, p.rank),
            vmem(p.rows, p.rank),
            vmem(p.rows, p.hcols),
            vmem(2 * p.ghalf, p.half),
            vmem(p.ghalf - p.gpiece, p.half),
            vmem(p.nx * p.gpiece, p.half),
            vmem(2 * p.ghalf, p.half),
            vmem(p.rank, p.rank),
            vmem(p.rank, p.hcols),
            vmem(A_CHUNKS, p.chunk - p.ax, p.hcols),
            vmem(A_CHUNKS, p.ax, p.hcols),
            vmem(A_CHUNKS, (p.ny - 1) * p.ay_rows, p.ay_cols),
            vmem(p.chunk - p.by, p.hcols),
            vmem(p.by, p.hcols),
            vmem((p.nx - 1) * p.bx_rows, p.bx_cols),
            vmem(p.rank, p.hcols),
            vmem(p.rank, p.rank),
            vmem(2, p.rank, p.hcols),
            vmem(2 * p.nz - 1, 1, p.rank),
            vmem(1, p.rank),
            pltpu.SemaphoreType.DMA((len(STAGES),)),
            pltpu.SemaphoreType.DMA((len(STAGES),)),
            pltpu.SemaphoreType.DMA((2,)),
        ],
        compiler_params=pltpu.CompilerParams(collective_id=0, has_side_effects=True, vmem_limit_bytes=VMEM_BYTES),
        name="dion",
    )(
        pltpu.with_memory_space_constraint(momentum, pltpu.HBM),
        pltpu.with_memory_space_constraint(right_factor, pltpu.HBM),
    )
    return pl.pallas_call(
        write_outputs,
        out_shape=(shaped(p.rows, p.cols),) * 2,
        in_specs=[vmem_spec] * 3,
        out_specs=(any_spec, any_spec),
        scratch_shapes=[vmem(p.rows, p.cols), pltpu.SemaphoreType.DMA((3,))],
        compiler_params=pltpu.CompilerParams(vmem_limit_bytes=8 * 2**20),
        name="outputs",
    )(new, right, left)


def solution(mesh):
    nz = mesh.shape["col"]
    ny = Y_CHIPS
    nx = mesh.shape["row"] // (ny * CORES)

    def local(momentum, right_factor):
        plan = Plan(nx, ny, nz, momentum.shape[0], momentum.shape[1], right_factor.shape[1])
        return local_step(plan, momentum, right_factor)

    in_specs = (P("row", "col"), P("col", None))
    out_specs = (P("row", "col"), P("row", "col"))
    return jax.shard_map(local, mesh=mesh, in_specs=in_specs, out_specs=out_specs, check_vma=False)
```
